32 devices in a mesh: groups: 2 (over x), ctx: 16 (over z, y, core).
Axes of the slice: x: 2, y: 2, z: 4, core: 2. Of those that a mesh axis runs over, the one named last changes fastest.
Arguments:
- mixer_input: bfloat16 [2048, 8192], P(('groups', 'ctx')), parts along dimension 0, may hold values from -6 to 6
- gate_input: bfloat16 [2048, 8192], P(('groups', 'ctx')), parts along dimension 0, may hold values from -6 to 6
- step_raw: bfloat16 [2048, 8192], P(('groups', 'ctx')), parts along dimension 0, may hold values from -4 to 4
- input_proj: float32 [2048, 16], P(('groups', 'ctx')), parts along dimension 0, may hold values from -0.6 to 0.6
- output_proj: float32 [2048, 16], P(('groups', 'ctx')), parts along dimension 0, may hold values from -1.8 to 1.8
- decay_log: float32 [8192, 16], replicated, may hold values from -12 to 0
- conv_weight: float32 [8192, 4], replicated, may hold values from -3 to 3
- conv_bias: float32 [8192], replicated, may hold values from -3 to 3
- skip_gain: float32 [8192], replicated, may hold values from 0.5 to 1.5
- query_heads: bfloat16 [2048, 4096], P(('groups', 'ctx')), parts along dimension 0, may hold values from -6 to 6
- key_heads: bfloat16 [2048, 512], P(('groups', 'ctx')), parts along dimension 0, may hold values from -4 to 4
- value_heads: bfloat16 [2048, 512], P(('groups', 'ctx')), parts along dimension 0, may hold values from -6 to 6
Outputs:
- mixer_output: bfloat16 [2048, 8192], P(('groups', 'ctx')), parts along dimension 0
- attention: bfloat16 [2048, 4096], P(('groups', 'ctx')), parts along dimension 0
The draws below stay inside these ranges and needn't reach their ends.
There are 2 independent parts, one for each index of `groups`. The reference program is written for one: setup_inputs(seed, part) draws one part's arguments, and reference() takes and returns one part's arrays. A program takes and returns all parts, laid end to end along the dimension named above; an argument that names none is the same for every part. Nothing has to cross between parts.
All inputs are finite; a program needn't handle non-finite values.
Results may differ from the reference program's by a relative error of at most 0.0085.
Values may be sent and summed in bfloat16 or wider, within the bound.
A program may use at most 320 MiB of HBM per device.

```python
import math
import jax
import jax.numpy as jnp
from jax import lax

CH = 8192
STATE = 16
TAPS = 4
Q_HEADS = 32
KV_HEADS = 4
HEAD_DIM = 128
TOK_DEV = 64
SEQ = 1024


def draw_query_heads(key, part):
    shape_all = (SEQ, Q_HEADS * HEAD_DIM)
    probe_readings = jnp.clip(jax.random.normal(jax.random.fold_in(key, 1), shape_all, jnp.float32), -4.0, 4.0)
    return probe_readings.astype(jnp.bfloat16)


def draw_key_heads(key, part):
    shape_all = (SEQ, KV_HEADS * HEAD_DIM)
    probe_readings = jnp.clip(jax.random.normal(jax.random.fold_in(key, 2), shape_all, jnp.float32), -4.0, 4.0)
    return probe_readings.astype(jnp.bfloat16)


def draw_decay_log(key, part):
    slow_share = 0.5
    slow_level = jnp.exp(jax.random.uniform(jax.random.fold_in(key, 23), (CH,), jnp.float32, jnp.log(0.2), jnp.log(0.4)))
    slow_rate = slow_level / (TOK_DEV * 0.8)
    slow_pick = jax.random.bernoulli(jax.random.fold_in(key, 21), slow_share, (CH,))
    fast_rate = jnp.exp(jax.random.uniform(jax.random.fold_in(key, 22), (CH,), jnp.float32, jnp.log(0.025), jnp.log(0.05)))
    spread = jax.random.uniform(jax.random.fold_in(key, 24), (CH, STATE), jnp.float32, -0.7, 0.7)
    chosen = jnp.where(slow_pick, slow_rate, fast_rate)
    return (jnp.log(chosen)[:, None] + spread).astype(jnp.float32)


def draw_step_raw(key, part):
    shape_all = (SEQ, CH)
    noise = jnp.clip(0.5 * jax.random.normal(jax.random.fold_in(key, 31), shape_all, jnp.float32), -2.5, 2.5)
    position_offsets = jax.random.uniform(jax.random.fold_in(key, 32), (SEQ // TOK_DEV,), jnp.float32, -1.0, 1.0)
    element_indices = jnp.arange(SEQ)
    probe_readings = noise + position_offsets[element_indices // TOK_DEV][:, None]
    probe_indices = jax.random.randint(jax.random.fold_in(key, 33), (4,), 0, SEQ)
    packet_clusters = jnp.any(element_indices[:, None] == probe_indices[None, :], axis=1)
    probe_readings = jnp.where(packet_clusters[:, None], 4.0, probe_readings)
    return probe_readings.astype(jnp.bfloat16)


def levels(stream_key, extent, shards, least, top_value):
    def one(position, blocks):
        steps = jax.random.uniform(jax.random.fold_in(jax.random.fold_in(stream_key, 6), position), (blocks,), jnp.float32, least / len(shards), top_value / len(shards))
        return jnp.repeat(jnp.exp(steps), extent[position] // blocks).reshape((-1,) + (1,) * (len(extent) - position - 1))

    level = one(*shards[0])
    for cut in shards[1:]:
        level = level * one(*cut)
    return level


def centred(own_key, shape, width, limit, split=(), kind=jnp.bfloat16):
    level = levels(own_key, shape, split, -0.22, 0.18) if split else 1.0
    drawn = jax.random.normal(own_key, shape, jnp.float32) * width * level
    return jnp.minimum(jnp.maximum(drawn, -limit), limit).astype(kind)


def setup_inputs(seed: int = 0, part: int = 0) -> dict:
    seeds = jax.random.split(jax.random.key(seed), 13)
    own_keys = jax.random.split(jax.random.fold_in(seeds[12], part), 13)
    return {
        "mixer_input": centred(own_keys[0], (SEQ, CH), 1.0, 6.0, ((0, 16),)),
        "gate_input": centred(own_keys[1], (SEQ, CH), 1.0, 6.0, ((0, 16),)),
        "step_raw": draw_step_raw(jax.random.fold_in(jax.random.fold_in(seeds[12], part), 71), part),
        "input_proj": centred(own_keys[3], (SEQ, STATE), 0.1, 0.6, ((0, 16),), jnp.float32),
        "output_proj": centred(own_keys[4], (SEQ, STATE), 0.3, 1.8, ((0, 16),), jnp.float32),
        "decay_log": draw_decay_log(jax.random.fold_in(seeds[12], 71), part),
        "conv_weight": centred(seeds[6], (CH, TAPS), TAPS ** -0.5, 3.0, (), jnp.float32),
        "conv_bias": centred(seeds[7], (CH,), 0.5, 3.0, (), jnp.float32),
        "skip_gain": jnp.clip(jax.random.uniform(seeds[8], (CH,), jnp.float32, 0.5, 1.5), 0.5, 1.5),
        "query_heads": draw_query_heads(jax.random.fold_in(jax.random.fold_in(seeds[12], part), 71), part),
        "key_heads": draw_key_heads(jax.random.fold_in(jax.random.fold_in(seeds[12], part), 71), part),
        "value_heads": centred(own_keys[11], (SEQ, KV_HEADS * HEAD_DIM), 1.0, 6.0, ((0, 16),)),
    }


def reference(mixer_input, gate_input, step_raw, input_proj, output_proj, decay_log, conv_weight, conv_bias, skip_gain, query_heads, key_heads, value_heads):
    padded = jnp.concatenate([jnp.zeros((TAPS - 1, CH), jnp.bfloat16), mixer_input], axis=0)
    conv_sum = jnp.zeros((SEQ, CH), jnp.float32) + conv_bias[None, :]
    for tap_index in range(TAPS):
        conv_sum = conv_sum + conv_weight[:, tap_index][None, :] * padded[tap_index:tap_index + SEQ].astype(jnp.float32)
    inner_act = jax.nn.silu(conv_sum)
    step_size = jax.nn.softplus(step_raw.astype(jnp.float32))
    decay_rates = -jnp.exp(decay_log)

    def step_forward(hidden_state, items):
        step_now, inner_now, b_row, c_row = items
        decay_now = jnp.exp(step_now[:, None] * decay_rates)
        hidden_state = decay_now * hidden_state + (step_now * inner_now)[:, None] * b_row[None, :]
        return (hidden_state, lax.optimization_barrier(jnp.sum(hidden_state * c_row[None, :], axis=1)))
    final_state, scanned = lax.scan(step_forward, jnp.zeros((CH, STATE), jnp.float32), (step_size, inner_act, input_proj, output_proj))
    mixer_output = ((scanned + skip_gain[None, :] * inner_act) * jax.nn.silu(gate_input.astype(jnp.float32))).astype(jnp.bfloat16)
    groups_per = Q_HEADS // KV_HEADS
    block_rows = math.gcd(SEQ, 512)
    score_scale = 1.0 / math.sqrt(HEAD_DIM)
    queries4 = query_heads.reshape(SEQ, KV_HEADS, groups_per, HEAD_DIM)
    keys3 = key_heads.reshape(SEQ, KV_HEADS, HEAD_DIM)
    values3 = value_heads.reshape(SEQ, KV_HEADS, HEAD_DIM)
    key_places = jnp.arange(SEQ)

    def one_block(block_index):
        first_row = block_index * block_rows
        asker_panel_height = lax.dynamic_slice_in_dim(queries4, first_row, block_rows, 0)
        query_places = first_row + jnp.arange(block_rows)
        allowed = key_places[None, None, :] <= query_places[:, None, None]

        def one_head(head_index):
            query_head = asker_panel_height[:, head_index].astype(jnp.float32)
            key_head = keys3[:, head_index].astype(jnp.float32)
            value_head = values3[:, head_index].astype(jnp.float32)
            scores = jnp.einsum('tgd,sd->tgs', query_head, key_head) * score_scale
            scores = jnp.where(allowed, scores, -1e+30)
            largest = lax.optimization_barrier(jnp.max(scores, axis=2, keepdims=True))
            probs = jnp.where(allowed, jnp.exp(scores - largest), 0.0)
            totals = lax.optimization_barrier(jnp.sum(probs, axis=2))
            rounded = probs.astype(jnp.bfloat16).astype(jnp.float32)
            summed = jnp.einsum('tgs,sd->tgd', rounded, value_head)
            return summed / totals[:, :, None]
        per_head = lax.map(one_head, jnp.arange(KV_HEADS))
        return jnp.transpose(per_head, (1, 0, 2, 3))
    blocks = lax.map(one_block, jnp.arange(SEQ // block_rows))
    attention = blocks.reshape(SEQ, Q_HEADS * HEAD_DIM).astype(jnp.bfloat16)
    return (mixer_output, attention)
```

```python
import math
from functools import partial

import jax
import jax.numpy as jnp
from jax import lax
from jax.experimental import pallas as pl
from jax.experimental.pallas import tpu as pltpu
from jax.sharding import PartitionSpec as P

STATE = 16
TAPS = 4
Q_HEADS = 32
KV_HEADS = 4
HEAD_DIM = 128
LANES = 128
SUB = 8
WIDE = SUB * LANES
MSG = 32
LOG2E = math.log2(math.e)


def silu(v):
    return v / (1.0 + jnp.exp(-v))


def first_pass(
    split, rim_ref, x_ref, raw_ref, w_ref, bias_ref, rate_ref, b_ref, step_ref, inner_ref, msg_ref, ext, fin
):
    rows = x_ref.shape[0]
    rim_rows = TAPS - 1
    ext[pl.ds(SUB - rim_rows, rim_rows), :] = rim_ref[...].astype(jnp.float32)
    ext[pl.ds(SUB, rows), :] = x_ref[...].astype(jnp.float32)
    for k in range(SUB):
        cols = pl.ds(k * LANES, LANES)
        conv = jnp.zeros((rows, LANES), jnp.float32) + bias_ref[:, cols]
        for tap in range(TAPS):
            conv = conv + w_ref[pl.ds(tap, 1), cols] * ext[pl.ds(SUB - rim_rows + tap, rows), cols]
        raw = raw_ref[:, cols].astype(jnp.float32)
        inner_ref[pl.ds(k, rows, stride=SUB), :] = silu(conv)
        step_ref[pl.ds(k, rows, stride=SUB), :] = jnp.maximum(raw, 0.0) + jnp.log1p(
            jnp.exp(-jnp.abs(raw))
        )
    rates = [rate_ref[pl.ds(n, SUB, stride=STATE), :] for n in range(STATE)]

    def one(t, carry):
        total, hs = carry
        step = step_ref[pl.ds(pl.multiple_of(t * SUB, SUB), SUB), :]
        u = step * inner_ref[pl.ds(pl.multiple_of(t * SUB, SUB), SUB), :]
        new = []
        for n in range(STATE):
            b = jnp.broadcast_to(b_ref[pl.ds(t * STATE + n, 1), :], (SUB, LANES))
            new.append(jnp.exp2(step * rates[n]) * hs[n] + u * b)
        return total + step, tuple(new)

    zero = jnp.zeros((SUB, LANES), jnp.float32)
    total, hs = lax.fori_loop(0, rows, one, (zero, (zero,) * STATE), unroll=2)
    per = STATE // split
    left = total
    pieces = []
    for n in range(per):
        piece = left.astype(jnp.bfloat16).astype(jnp.float32)
        pieces.append(piece)
        left = left - piece
    for part in range(split):
        for n in range(per):
            row = part * 2 * per + n
            fin[pl.ds(row, SUB, stride=MSG), :] = hs[part * per + n]
            fin[pl.ds(row + per, SUB, stride=MSG), :] = pieces[n]
    msg_ref[...] = fin[...].astype(jnp.bfloat16)


def join_pass(size, split, got_ref, rate_ref, ent_ref):
    per = STATE // split
    units = rate_ref.shape[0] // per
    for k in range(units):
        rate = rate_ref[pl.ds(k * per, per), :]
        h = jnp.zeros((per, LANES), jnp.float32)
        for d in range(size):
            ent_ref[pl.ds((d * units + k) * per, per), :] = h.astype(jnp.bfloat16)
            at = (d * units + k) * 2 * per
            own = got_ref[pl.ds(at, per), :].astype(jnp.float32)
            parts = got_ref[pl.ds(at + per, per), :].astype(jnp.float32)
            total = (parts[0:1] + parts[1:2]) + parts[2:3]
            h = jnp.exp2(rate * total) * h + own


def second_pass(
    step_ref, inner_ref, gate_ref, skip_ref, rate_ref, b_ref, c_ref, ent_ref, out_ref, ent, ysc
):
    rows = gate_ref.shape[0]
    ent[...] = ent_ref[...].astype(jnp.float32)
    rates = [rate_ref[pl.ds(n, SUB, stride=STATE), :] for n in range(STATE)]
    start = tuple(ent[pl.ds(n, SUB, stride=STATE), :] for n in range(STATE))
    skip = skip_ref[...]

    def one(t, hs):
        at = pl.ds(pl.multiple_of(t * SUB, SUB), SUB)
        step = step_ref[at, :]
        inner = inner_ref[at, :]
        u = step * inner
        sums = [skip * inner, None]
        new = []
        for n in range(STATE):
            row = pl.ds(t * STATE + n, 1)
            b = jnp.broadcast_to(b_ref[row, :], (SUB, LANES))
            c = jnp.broadcast_to(c_ref[row, :], (SUB, LANES))
            h = jnp.exp2(step * rates[n]) * hs[n] + u * b
            new.append(h)
            term = h * c
            sums[n % 2] = term if sums[n % 2] is None else sums[n % 2] + term
        ysc[at, :] = sums[0] + sums[1]
        return tuple(new)

    lax.fori_loop(0, rows, one, start, unroll=2)
    for k in range(SUB):
        cols = pl.ds(k * LANES, LANES)
        y = ysc[pl.ds(k, rows, stride=SUB), :]
        out_ref[:, cols] = (y * silu(gate_ref[:, cols].astype(jnp.float32))).astype(jnp.bfloat16)


def attend(place_ref, q_ref, k_ref, v_ref, out_ref):
    rows = q_ref.shape[0]
    keys = k_ref.shape[0]
    heads = q_ref.shape[1] // HEAD_DIM
    chunk = math.gcd(keys, 1024)
    scale = LOG2E / math.sqrt(HEAD_DIM)
    q = jnp.concatenate([q_ref[:, pl.ds(h * HEAD_DIM, HEAD_DIM)] for h in range(heads)], axis=0)

    def fold(first, running):
        at = pl.ds(first, chunk)
        scores = lax.dot_general(
            q, k_ref[at, :], (((1,), (1,)), ((), ())), preferred_element_type=jnp.float32
        ).reshape(heads, rows, chunk)
        place = place_ref[0] + lax.broadcasted_iota(jnp.int32, (1, rows, chunk), 1)
        allowed = first + lax.broadcasted_iota(jnp.int32, (1, rows, chunk), 2) <= place
        scores = jnp.where(allowed, scores, -1e30)
        largest = jnp.max(scores, axis=2, keepdims=True)
        if running is not None:
            largest = jnp.maximum(largest, running[0])
        probs = jnp.exp2((scores - largest) * scale)
        totals = jnp.sum(probs, axis=2, keepdims=True)
        summed = jnp.dot(
            probs.reshape(heads * rows, chunk).astype(jnp.bfloat16),
            v_ref[at, :],
            preferred_element_type=jnp.float32,
        ).reshape(heads, rows, HEAD_DIM)
        if running is not None:
            shrink = jnp.exp2((running[0] - largest) * scale)
            totals = totals + running[1] * shrink
            summed = summed + running[2] * shrink
        return largest, totals, summed

    running = fold(0, None)
    if keys > chunk:
        running = lax.fori_loop(
            1,
            keys // chunk,
            lambda i, held: fold(pl.multiple_of(i * chunk, chunk), held),
            running,
        )
    out = (running[2] / running[1]).astype(jnp.bfloat16)
    for h in range(heads):
        out_ref[:, pl.ds(h * HEAD_DIM, HEAD_DIM)] = out[h]


def full(shape):
    return pl.BlockSpec(shape, lambda *_: (0,) * len(shape))


def per_device(
    mixer_input,
    gate_input,
    step_raw,
    input_proj,
    output_proj,
    decay_log,
    conv_weight,
    conv_bias,
    skip_gain,
    query_heads,
    key_heads,
    value_heads,
):
    rows, channels = mixer_input.shape
    size = lax.axis_size("ctx")
    own = lax.axis_index("ctx")
    groups = channels // WIDE
    split = max(1, size // (channels // LANES))
    tiles = channels // LANES
    f32, bf16 = jnp.float32, jnp.bfloat16
    shape = jax.ShapeDtypeStruct

    rim = lax.ppermute(
        mixer_input[rows - (TAPS - 1) :], "ctx", [(i, i + 1) for i in range(size - 1)]
    )
    pairs = lax.all_gather(
        jnp.concatenate([key_heads, value_heads], axis=1), "ctx", axis=0, tiled=True
    )
    rates = -LOG2E * jnp.exp(decay_log)
    rates = rates.reshape(tiles, LANES, STATE).transpose(0, 2, 1).reshape(tiles * STATE, LANES)
    b_rows = jnp.broadcast_to(input_proj.reshape(-1, 1), (rows * STATE, LANES))
    c_rows = jnp.broadcast_to(output_proj.reshape(-1, 1), (rows * STATE, LANES))

    wide = pl.BlockSpec((rows, WIDE), lambda g: (0, g))
    slab = pl.BlockSpec((None, rows * SUB, LANES), lambda g: (g, 0, 0))
    rate_spec = pl.BlockSpec((SUB * STATE, LANES), lambda g: (g, 0))
    slab_shape = shape((groups, rows * SUB, LANES), f32)
    step, inner, message = pl.pallas_call(
        partial(first_pass, split),
        grid=(groups,),
        in_specs=[
            pl.BlockSpec((TAPS - 1, WIDE), lambda g: (0, g)),
            wide,
            wide,
            pl.BlockSpec((TAPS, WIDE), lambda g: (0, g)),
            pl.BlockSpec((1, WIDE), lambda g: (0, g)),
            rate_spec,
            full((rows * STATE, LANES)),
        ],
        out_specs=[slab, slab, pl.BlockSpec((SUB * MSG, LANES), lambda g: (g, 0))],
        out_shape=[slab_shape, slab_shape, shape((tiles * MSG, LANES), bf16)],
        scratch_shapes=[
            pltpu.VMEM((SUB + rows, WIDE), f32),
            pltpu.VMEM((SUB * MSG, LANES), f32),
        ],
        cost_estimate=pl.CostEstimate(
            flops=6 * rows * channels * STATE,
            bytes_accessed=8 * rows * channels,
            transcendentals=rows * channels * STATE,
        ),
        name="first_pass",
    )(rim, mixer_input, step_raw, conv_weight.T, conv_bias[None], rates, b_rows)

    got = lax.all_to_all(message, "ctx", 0, 0, tiled=True)
    share = tiles * STATE // size
    own_rates = lax.dynamic_slice_in_dim(rates, own * share, share, 0)
    answers = pl.pallas_call(
        partial(join_pass, size, split),
        out_shape=shape((tiles * STATE, LANES), bf16),
        name="join_pass",
    )(got, own_rates)
    entering = lax.all_to_all(answers, "ctx", 0, 0, tiled=True)

    panel = Q_HEADS // KV_HEADS * HEAD_DIM
    keys = rows * size
    attention = pl.pallas_call(
        attend,
        grid=(KV_HEADS,),
        in_specs=[
            pl.BlockSpec(memory_space=pltpu.SMEM),
            pl.BlockSpec((rows, panel), lambda g: (0, g)),
            pl.BlockSpec((keys, HEAD_DIM), lambda g: (0, g)),
            pl.BlockSpec((keys, HEAD_DIM), lambda g: (0, KV_HEADS + g)),
        ],
        out_specs=pl.BlockSpec((rows, panel), lambda g: (0, g)),
        out_shape=shape((rows, Q_HEADS * HEAD_DIM), bf16),
        cost_estimate=pl.CostEstimate(
            flops=4 * rows * Q_HEADS * keys * HEAD_DIM,
            bytes_accessed=4 * keys * KV_HEADS * HEAD_DIM,
            transcendentals=rows * Q_HEADS * keys,
        ),
        name="attend",
    )((own * rows).astype(jnp.int32)[None], query_heads, pairs, pairs)

    mixer_output = pl.pallas_call(
        second_pass,
        grid=(groups,),
        in_specs=[
            slab,
            slab,
            wide,
            pl.BlockSpec((SUB, LANES), lambda g: (g, 0)),
            rate_spec,
            full((rows * STATE, LANES)),
            full((rows * STATE, LANES)),
            rate_spec,
        ],
        out_specs=wide,
        out_shape=shape((rows, channels), bf16),
        scratch_shapes=[
            pltpu.VMEM((SUB * STATE, LANES), f32),
            pltpu.VMEM((rows * SUB, LANES), f32),
        ],
        cost_estimate=pl.CostEstimate(
            flops=8 * rows * channels * STATE,
            bytes_accessed=12 * rows * channels,
            transcendentals=rows * channels * STATE,
        ),
        name="second_pass",
    )(step, inner, gate_input, skip_gain.reshape(tiles, LANES), rates, b_rows, c_rows, entering)
    return (mixer_output, attention)


def solution(mesh):
    tokens = P(("groups", "ctx"), None)
    in_specs = (tokens,) * 5 + (P(),) * 4 + (tokens,) * 3
    return jax.shard_map(
        per_device, mesh=mesh, in_specs=in_specs, out_specs=(tokens, tokens), check_vma=False
    )
```

```python
import math

import jax
import jax.numpy as jnp
from jax import lax
from jax.experimental import pallas as pl
from jax.experimental.pallas import tpu as pltpu
from jax.sharding import PartitionSpec as P

STATE = 16
TAPS = 4
Q_HEADS = 32
KV_HEADS = 4
HEAD_DIM = 128
LANES = 128
SUB = 8
WIDE = SUB * LANES
HEAD = 16
LOG2E = math.log2(math.e)


def silu(v):
    return v / (1.0 + jnp.exp(-v))


def first_pass(
    rim_ref, x_ref, raw_ref, w_ref, bias_ref, rate_ref, b_ref, step_ref, inner_ref, fin_ref, tot_ref,
    ext, fin
):
    rows = x_ref.shape[0]
    rim_rows = TAPS - 1
    ext[pl.ds(SUB - rim_rows, rim_rows), :] = rim_ref[...].astype(jnp.float32)
    ext[pl.ds(SUB, rows), :] = x_ref[...].astype(jnp.float32)
    for k in range(SUB):
        cols = pl.ds(k * LANES, LANES)
        conv = jnp.zeros((rows, LANES), jnp.float32) + bias_ref[:, cols]
        for tap in range(TAPS):
            conv = conv + w_ref[pl.ds(tap, 1), cols] * ext[pl.ds(SUB - rim_rows + tap, rows), cols]
        raw = raw_ref[:, cols].astype(jnp.float32)
        inner_ref[pl.ds(k, rows, stride=SUB), :] = silu(conv)
        step_ref[pl.ds(k, rows, stride=SUB), :] = jnp.maximum(raw, 0.0) + jnp.log1p(
            jnp.exp(-jnp.abs(raw))
        )
    rates = [rate_ref[pl.ds(n, SUB, stride=STATE), :] for n in range(STATE)]

    def one(t, carry):
        total, hs = carry
        step = step_ref[pl.ds(pl.multiple_of(t * SUB, SUB), SUB), :]
        u = step * inner_ref[pl.ds(pl.multiple_of(t * SUB, SUB), SUB), :]
        new = []
        for n in range(STATE):
            b = jnp.broadcast_to(b_ref[pl.ds(t * STATE + n, 1), :], (SUB, LANES))
            new.append(jnp.exp2(step * rates[n]) * hs[n] + u * b)
        return total + step, tuple(new)

    zero = jnp.zeros((SUB, LANES), jnp.float32)
    total, hs = lax.fori_loop(0, rows, one, (zero, (zero,) * STATE), unroll=2)
    for n in range(STATE):
        fin[pl.ds(n, SUB, stride=STATE), :] = hs[n]
    fin_ref[...] = fin[...].astype(jnp.bfloat16)
    tot_ref[...] = total


def exchange(
    fin_ref, tot_ref, rate_ref, ent_ref, snd, got, ans, lands, send_a, recv_a, send_b, recv_b
):
    size, share, _ = ans.shape
    tiles = tot_ref.shape[0]
    count = max(1, tiles // size)
    per = share // count
    me = lax.axis_index("ctx")
    barrier = pltpu.get_barrier_semaphore()

    def greet(off, _):
        pl.semaphore_signal(
            barrier,
            inc=1,
            device_id={"ctx": lax.rem(me + off, size)},
            device_id_type=pl.DeviceIdType.MESH,
        )
        return 0

    lax.fori_loop(1, size, greet, 0)
    filler = jnp.zeros((HEAD - 3 * count, LANES), jnp.float32)
    for j in range(size):
        left = tot_ref[pl.ds(j * tiles // size, count), :]
        pieces = []
        for _ in range(3):
            pieces.append(left.astype(jnp.bfloat16).astype(jnp.float32))
            left = left - pieces[-1]
        snd[j, pl.ds(0, HEAD), :] = jnp.concatenate(pieces + [filler], axis=0).astype(jnp.bfloat16)
        snd[j, pl.ds(HEAD, share), :] = fin_ref[pl.ds(j * share, share), :]
    pl.semaphore_wait(barrier, size - 1)

    def ask(to, origin):
        return pltpu.make_async_remote_copy(
            src_ref=snd.at[to],
            dst_ref=got.at[origin],
            send_sem=send_a.at[to],
            recv_sem=recv_a.at[origin],
            device_id={"ctx": to},
            device_id_type=pl.DeviceIdType.MESH,
        )

    def answer(to, origin):
        return pltpu.make_async_remote_copy(
            src_ref=ans.at[to],
            dst_ref=lands.at[origin],
            send_sem=send_b.at[to],
            recv_sem=recv_b.at[origin],
            device_id={"ctx": to},
            device_id_type=pl.DeviceIdType.MESH,
        )

    def start_ask(off, _):
        ask(lax.rem(me + off, size), me).start()
        return 0

    lax.fori_loop(1, size, start_ask, 0)
    got[me] = snd[me]

    def join(d, hs):
        @pl.when(d != me)
        def _():
            ask(d, d).wait_recv()

        parts = got[d, pl.ds(0, HEAD), :].astype(jnp.float32)
        new = []
        for k in range(count):
            ans[d, pl.ds(k * per, per), :] = hs[k].astype(jnp.bfloat16)
            total = (
                parts[k : k + 1] + parts[count + k : count + k + 1]
            ) + parts[2 * count + k : 2 * count + k + 1]
            rate = rate_ref[pl.ds(pl.multiple_of(me * share + k * per, SUB), per), :]
            own = got[d, pl.ds(HEAD + k * per, per), :].astype(jnp.float32)
            new.append(jnp.exp2(rate * total) * hs[k] + own)

        @pl.when(d != me)
        def _():
            answer(d, me).start()

        return tuple(new)

    lax.fori_loop(0, size, join, (jnp.zeros((per, LANES), jnp.float32),) * count)
    lands[me] = ans[me]

    def finish(off, _):
        other = lax.rem(me + off, size)
        answer(other, other).wait_recv()
        ask(other, other).wait_send()
        answer(other, other).wait_send()
        return 0

    lax.fori_loop(1, size, finish, 0)
    ent_ref[...] = lands[...]


def second_pass(
    step_ref, inner_ref, gate_ref, skip_ref, rate_ref, b_ref, c_ref, ent_ref, out_ref, ent, ysc
):
    rows = gate_ref.shape[0]
    ent[...] = ent_ref[...].astype(jnp.float32)
    rates = [rate_ref[pl.ds(n, SUB, stride=STATE), :] for n in range(STATE)]
    start = tuple(ent[pl.ds(n, SUB, stride=STATE), :] for n in range(STATE))
    skip = skip_ref[...]

    def one(t, hs):
        at = pl.ds(pl.multiple_of(t * SUB, SUB), SUB)
        step = step_ref[at, :]
        inner = inner_ref[at, :]
        u = step * inner
        sums = [skip * inner, None]
        new = []
        for n in range(STATE):
            row = pl.ds(t * STATE + n, 1)
            b = jnp.broadcast_to(b_ref[row, :], (SUB, LANES))
            c = jnp.broadcast_to(c_ref[row, :], (SUB, LANES))
            h = jnp.exp2(step * rates[n]) * hs[n] + u * b
            new.append(h)
            term = h * c
            sums[n % 2] = term if sums[n % 2] is None else sums[n % 2] + term
        ysc[at, :] = sums[0] + sums[1]
        return tuple(new)

    lax.fori_loop(0, rows, one, start, unroll=2)
    for k in range(SUB):
        cols = pl.ds(k * LANES, LANES)
        y = ysc[pl.ds(k, rows, stride=SUB), :]
        out_ref[:, cols] = (y * silu(gate_ref[:, cols].astype(jnp.float32))).astype(jnp.bfloat16)


def attend(place_ref, q_ref, k_ref, v_ref, out_ref):
    rows = q_ref.shape[0]
    keys = k_ref.shape[0]
    heads = q_ref.shape[1] // HEAD_DIM
    chunk = math.gcd(keys, 1024)
    scale = LOG2E / math.sqrt(HEAD_DIM)
    q = jnp.concatenate([q_ref[:, pl.ds(h * HEAD_DIM, HEAD_DIM)] for h in range(heads)], axis=0)

    def fold(first, running):
        at = pl.ds(first, chunk)
        scores = lax.dot_general(
            q, k_ref[at, :], (((1,), (1,)), ((), ())), preferred_element_type=jnp.float32
        ).reshape(heads, rows, chunk)
        place = place_ref[0] + lax.broadcasted_iota(jnp.int32, (1, rows, chunk), 1)
        allowed = first + lax.broadcasted_iota(jnp.int32, (1, rows, chunk), 2) <= place
        scores = jnp.where(allowed, scores, -1e30)
        largest = jnp.max(scores, axis=2, keepdims=True)
        if running is not None:
            largest = jnp.maximum(largest, running[0])
        probs = jnp.exp2((scores - largest) * scale)
        totals = jnp.sum(probs, axis=2, keepdims=True)
        summed = jnp.dot(
            probs.reshape(heads * rows, chunk).astype(jnp.bfloat16),
            v_ref[at, :],
            preferred_element_type=jnp.float32,
        ).reshape(heads, rows, HEAD_DIM)
        if running is not None:
            shrink = jnp.exp2((running[0] - largest) * scale)
            totals = totals + running[1] * shrink
            summed = summed + running[2] * shrink
        return largest, totals, summed

    running = fold(0, None)
    if keys > chunk:
        running = lax.fori_loop(
            1,
            keys // chunk,
            lambda i, held: fold(pl.multiple_of(i * chunk, chunk), held),
            running,
        )
    out = (running[2] / running[1]).astype(jnp.bfloat16)
    for h in range(heads):
        out_ref[:, pl.ds(h * HEAD_DIM, HEAD_DIM)] = out[h]


def full(shape):
    return pl.BlockSpec(shape, lambda *_: (0,) * len(shape))


def per_device(
    mixer_input,
    gate_input,
    step_raw,
    input_proj,
    output_proj,
    decay_log,
    conv_weight,
    conv_bias,
    skip_gain,
    query_heads,
    key_heads,
    value_heads,
):
    rows, channels = mixer_input.shape
    size = lax.axis_size("ctx")
    own = lax.axis_index("ctx")
    groups = channels // WIDE
    tiles = channels // LANES
    f32, bf16 = jnp.float32, jnp.bfloat16
    shape = jax.ShapeDtypeStruct

    rim = lax.ppermute(
        mixer_input[rows - (TAPS - 1) :], "ctx", [(i, i + 1) for i in range(size - 1)]
    )
    pairs = lax.all_gather(
        jnp.concatenate([key_heads, value_heads], axis=1), "ctx", axis=0, tiled=True
    )
    rates = -LOG2E * jnp.exp(decay_log)
    rates = rates.reshape(tiles, LANES, STATE).transpose(0, 2, 1).reshape(tiles * STATE, LANES)
    b_rows = jnp.broadcast_to(input_proj.reshape(-1, 1), (rows * STATE, LANES))
    c_rows = jnp.broadcast_to(output_proj.reshape(-1, 1), (rows * STATE, LANES))

    wide = pl.BlockSpec((rows, WIDE), lambda g: (0, g))
    slab = pl.BlockSpec((None, rows * SUB, LANES), lambda g: (g, 0, 0))
    rate_spec = pl.BlockSpec((SUB * STATE, LANES), lambda g: (g, 0))
    slab_shape = shape((groups, rows * SUB, LANES), f32)
    step, inner, finals, totals = pl.pallas_call(
        first_pass,
        grid=(groups,),
        in_specs=[
            pl.BlockSpec((TAPS - 1, WIDE), lambda g: (0, g)),
            wide,
            wide,
            pl.BlockSpec((TAPS, WIDE), lambda g: (0, g)),
            pl.BlockSpec((1, WIDE), lambda g: (0, g)),
            rate_spec,
            full((rows * STATE, LANES)),
        ],
        out_specs=[
            slab,
            slab,
            rate_spec,
            pl.BlockSpec((SUB, LANES), lambda g: (g, 0)),
        ],
        out_shape=[
            slab_shape,
            slab_shape,
            shape((tiles * STATE, LANES), bf16),
            shape((tiles, LANES), f32),
        ],
        scratch_shapes=[
            pltpu.VMEM((SUB + rows, WIDE), f32),
            pltpu.VMEM((SUB * STATE, LANES), f32),
        ],
        cost_estimate=pl.CostEstimate(
            flops=6 * rows * channels * STATE,
            bytes_accessed=8 * rows * channels,
            transcendentals=rows * channels * STATE,
        ),
        name="first_pass",
    )(rim, mixer_input, step_raw, conv_weight.T, conv_bias[None], rates, b_rows)

    share = tiles * STATE // size
    entering = pl.pallas_call(
        exchange,
        in_specs=[pl.BlockSpec(memory_space=pltpu.VMEM)] * 3,
        out_specs=pl.BlockSpec(memory_space=pltpu.VMEM),
        out_shape=shape((size, share, LANES), bf16),
        scratch_shapes=[
            pltpu.VMEM((size, HEAD + share, LANES), bf16),
            pltpu.VMEM((size, HEAD + share, LANES), bf16),
            pltpu.VMEM((size, share, LANES), bf16),
            pltpu.VMEM((size, share, LANES), bf16),
        ]
        + [pltpu.SemaphoreType.DMA((size,))] * 4,
        compiler_params=pltpu.CompilerParams(collective_id=0, has_side_effects=True),
        name="exchange",
    )(finals, totals, rates).reshape(tiles * STATE, LANES)

    panel = Q_HEADS // KV_HEADS * HEAD_DIM
    keys = rows * size
    attention = pl.pallas_call(
        attend,
        grid=(KV_HEADS,),
        in_specs=[
            pl.BlockSpec(memory_space=pltpu.SMEM),
            pl.BlockSpec((rows, panel), lambda g: (0, g)),
            pl.BlockSpec((keys, HEAD_DIM), lambda g: (0, g)),
            pl.BlockSpec((keys, HEAD_DIM), lambda g: (0, KV_HEADS + g)),
        ],
        out_specs=pl.BlockSpec((rows, panel), lambda g: (0, g)),
        out_shape=shape((rows, Q_HEADS * HEAD_DIM), bf16),
        cost_estimate=pl.CostEstimate(
            flops=4 * rows * Q_HEADS * keys * HEAD_DIM,
            bytes_accessed=4 * keys * KV_HEADS * HEAD_DIM,
            transcendentals=rows * Q_HEADS * keys,
        ),
        name="attend",
    )((own * rows).astype(jnp.int32)[None], query_heads, pairs, pairs)

    mixer_output = pl.pallas_call(
        second_pass,
        grid=(groups,),
        in_specs=[
            slab,
            slab,
            wide,
            pl.BlockSpec((SUB, LANES), lambda g: (g, 0)),
            rate_spec,
            full((rows * STATE, LANES)),
            full((rows * STATE, LANES)),
            rate_spec,
        ],
        out_specs=wide,
        out_shape=shape((rows, channels), bf16),
        scratch_shapes=[
            pltpu.VMEM((SUB * STATE, LANES), f32),
            pltpu.VMEM((rows * SUB, LANES), f32),
        ],
        cost_estimate=pl.CostEstimate(
            flops=8 * rows * channels * STATE,
            bytes_accessed=12 * rows * channels,
            transcendentals=rows * channels * STATE,
        ),
        name="second_pass",
    )(step, inner, gate_input, skip_gain.reshape(tiles, LANES), rates, b_rows, c_rows, entering)
    return (mixer_output, attention)


def solution(mesh):
    tokens = P(("groups", "ctx"), None)
    in_specs = (tokens,) * 5 + (P(),) * 4 + (tokens,) * 3
    return jax.shard_map(
        per_device, mesh=mesh, in_specs=in_specs, out_specs=(tokens, tokens), check_vma=False
    )
```

```python
import math

import jax
import jax.numpy as jnp
from jax import lax
from jax.experimental import pallas as pl
from jax.experimental.pallas import tpu as pltpu
from jax.sharding import PartitionSpec as P

STATE = 16
TAPS = 4
Q_HEADS = 32
KV_HEADS = 4
HEAD_DIM = 128
LANES = 128
SUB = 8
WIDE = SUB * LANES
HEAD = 16
LOG2E = math.log2(math.e)


def silu(v):
    return v / (1.0 + jnp.exp(-v))


def first_pass(
    rim_ref, x_ref, raw_ref, w_ref, bias_ref, rate_ref, b_ref, all_rates_ref,
    step_ref, inner_ref, ent_ref, ext, fin, snd, got, ans, lands, send_a, recv_a, send_b, recv_b
):
    size, share, _ = ans.shape
    group = pl.program_id(0)
    groups = pl.num_programs(0)
    share_count = STATE * SUB // share
    count = max(1, SUB // share_count)
    per = share // count
    me = lax.axis_index("ctx")
    barrier = pltpu.get_barrier_semaphore()

    def greet(off, _):
        pl.semaphore_signal(
            barrier,
            inc=1,
            device_id={"ctx": lax.rem(me + off, size)},
            device_id_type=pl.DeviceIdType.MESH,
        )
        return 0

    @pl.when(group == 0)
    def _():
        lax.fori_loop(1, size, greet, 0)

    def ask(to, origin):
        return pltpu.make_async_remote_copy(
            src_ref=snd.at[to],
            dst_ref=got.at[origin],
            send_sem=send_a.at[to],
            recv_sem=recv_a.at[origin],
            device_id={"ctx": to},
            device_id_type=pl.DeviceIdType.MESH,
        )

    def answer(to, origin):
        return pltpu.make_async_remote_copy(
            src_ref=ans.at[to],
            dst_ref=lands.at[origin],
            send_sem=send_b.at[to],
            recv_sem=recv_b.at[origin],
            device_id={"ctx": to},
            device_id_type=pl.DeviceIdType.MESH,
        )

    rows = x_ref.shape[0]
    rim_rows = TAPS - 1
    ext[pl.ds(SUB - rim_rows, rim_rows), :] = rim_ref[...].astype(jnp.float32)
    ext[pl.ds(SUB, rows), :] = x_ref[...].astype(jnp.float32)
    for k in range(SUB):
        cols = pl.ds(k * LANES, LANES)
        conv = jnp.zeros((rows, LANES), jnp.float32) + bias_ref[:, cols]
        for tap in range(TAPS):
            conv = conv + w_ref[pl.ds(tap, 1), cols] * ext[pl.ds(SUB - rim_rows + tap, rows), cols]
        raw = raw_ref[:, cols].astype(jnp.float32)
        inner_ref[pl.ds(k, rows, stride=SUB), :] = silu(conv)
        step_ref[pl.ds(k, rows, stride=SUB), :] = jnp.maximum(raw, 0.0) + jnp.log1p(
            jnp.exp(-jnp.abs(raw))
        )
    rates = [rate_ref[pl.ds(n, SUB, stride=STATE), :] for n in range(STATE)]

    def one(t, carry):
        total, hs = carry
        step = step_ref[pl.ds(pl.multiple_of(t * SUB, SUB), SUB), :]
        u = step * inner_ref[pl.ds(pl.multiple_of(t * SUB, SUB), SUB), :]
        new = []
        for n in range(STATE):
            b = jnp.broadcast_to(b_ref[pl.ds(t * STATE + n, 1), :], (SUB, LANES))
            new.append(jnp.exp2(step * rates[n]) * hs[n] + u * b)
        return total + step, tuple(new)

    zero = jnp.zeros((SUB, LANES), jnp.float32)
    total, hs = lax.fori_loop(0, rows, one, (zero, (zero,) * STATE), unroll=2)
    for n in range(STATE):
        fin[pl.ds(n, SUB, stride=STATE), :] = hs[n]

    @pl.when(group == 0)
    def _():
        pl.semaphore_wait(barrier, size - 1)

    filler = jnp.zeros((HEAD - 3 * count, LANES), jnp.float32)
    for part in range(share_count):
        to = group * share_count + part
        first = part * SUB // share_count
        left = total[first : first + count]
        pieces = []
        for _ in range(3):
            pieces.append(left.astype(jnp.bfloat16).astype(jnp.float32))
            left = left - pieces[-1]
        snd[to, pl.ds(0, HEAD), :] = jnp.concatenate(pieces + [filler], axis=0).astype(jnp.bfloat16)
        snd[to, pl.ds(HEAD, share), :] = fin[pl.ds(part * share, share), :].astype(jnp.bfloat16)

        @pl.when(to != me)
        def _():
            ask(to, me).start()

    def join(d, hs):
        @pl.when(d != me)
        def _():
            ask(d, d).wait_recv()

        parts = got[d, pl.ds(0, HEAD), :].astype(jnp.float32)
        new = []
        for k in range(count):
            ans[d, pl.ds(k * per, per), :] = hs[k].astype(jnp.bfloat16)
            total = (
                parts[k : k + 1] + parts[count + k : count + k + 1]
            ) + parts[2 * count + k : 2 * count + k + 1]
            rate = all_rates_ref[pl.ds(pl.multiple_of(me * share + k * per, SUB), per), :]
            own = got[d, pl.ds(HEAD + k * per, per), :].astype(jnp.float32)
            new.append(jnp.exp2(rate * total) * hs[k] + own)

        @pl.when(d != me)
        def _():
            answer(d, me).start()

        return tuple(new)

    @pl.when(group == jnp.minimum(me // share_count + 2, groups - 1))
    def _():
        got[me] = snd[me]
        lax.fori_loop(0, size, join, (jnp.zeros((per, LANES), jnp.float32),) * count)
        lands[me] = ans[me]

    def finish(off, _):
        other = lax.rem(me + off, size)
        answer(other, other).wait_recv()
        ask(other, other).wait_send()
        answer(other, other).wait_send()
        return 0

    @pl.when(group == groups - 1)
    def _():
        lax.fori_loop(1, size, finish, 0)
        ent_ref[...] = lands[...]


def second_pass(
    step_ref, inner_ref, gate_ref, skip_ref, rate_ref, b_ref, c_ref, ent_ref, out_ref, ent, ysc
):
    rows = gate_ref.shape[0]
    ent[...] = ent_ref[...].astype(jnp.float32)
    rates = [rate_ref[pl.ds(n, SUB, stride=STATE), :] for n in range(STATE)]
    start = tuple(ent[pl.ds(n, SUB, stride=STATE), :] for n in range(STATE))
    skip = skip_ref[...]

    def one(t, hs):
        at = pl.ds(pl.multiple_of(t * SUB, SUB), SUB)
        step = step_ref[at, :]
        inner = inner_ref[at, :]
        u = step * inner
        sums = [skip * inner, None]
        new = []
        for n in range(STATE):
            row = pl.ds(t * STATE + n, 1)
            b = jnp.broadcast_to(b_ref[row, :], (SUB, LANES))
            c = jnp.broadcast_to(c_ref[row, :], (SUB, LANES))
            h = jnp.exp2(step * rates[n]) * hs[n] + u * b
            new.append(h)
            term = h * c
            sums[n % 2] = term if sums[n % 2] is None else sums[n % 2] + term
        ysc[at, :] = sums[0] + sums[1]
        return tuple(new)

    lax.fori_loop(0, rows, one, start, unroll=2)
    for k in range(SUB):
        cols = pl.ds(k * LANES, LANES)
        y = ysc[pl.ds(k, rows, stride=SUB), :]
        out_ref[:, cols] = (y * silu(gate_ref[:, cols].astype(jnp.float32))).astype(jnp.bfloat16)


def attend(place_ref, q_ref, k_ref, v_ref, out_ref):
    rows = q_ref.shape[0]
    keys = k_ref.shape[0]
    heads = q_ref.shape[1] // HEAD_DIM
    chunk = math.gcd(keys, 1024)
    scale = LOG2E / math.sqrt(HEAD_DIM)
    q = jnp.concatenate([q_ref[:, pl.ds(h * HEAD_DIM, HEAD_DIM)] for h in range(heads)], axis=0)

    def fold(first, running):
        at = pl.ds(first, chunk)
        scores = lax.dot_general(
            q, k_ref[at, :], (((1,), (1,)), ((), ())), preferred_element_type=jnp.float32
        ).reshape(heads, rows, chunk)
        place = place_ref[0] + lax.broadcasted_iota(jnp.int32, (1, rows, chunk), 1)
        allowed = first + lax.broadcasted_iota(jnp.int32, (1, rows, chunk), 2) <= place
        scores = jnp.where(allowed, scores, -1e30)
        largest = jnp.max(scores, axis=2, keepdims=True)
        if running is not None:
            largest = jnp.maximum(largest, running[0])
        probs = jnp.exp2((scores - largest) * scale)
        totals = jnp.sum(probs, axis=2, keepdims=True)
        summed = jnp.dot(
            probs.reshape(heads * rows, chunk).astype(jnp.bfloat16),
            v_ref[at, :],
            preferred_element_type=jnp.float32,
        ).reshape(heads, rows, HEAD_DIM)
        if running is not None:
            shrink = jnp.exp2((running[0] - largest) * scale)
            totals = totals + running[1] * shrink
            summed = summed + running[2] * shrink
        return largest, totals, summed

    running = fold(0, None)
    if keys > chunk:
        running = lax.fori_loop(
            1,
            keys // chunk,
            lambda i, held: fold(pl.multiple_of(i * chunk, chunk), held),
            running,
        )
    out = (running[2] / running[1]).astype(jnp.bfloat16)
    for h in range(heads):
        out_ref[:, pl.ds(h * HEAD_DIM, HEAD_DIM)] = out[h]


def per_device(
    mixer_input,
    gate_input,
    step_raw,
    input_proj,
    output_proj,
    decay_log,
    conv_weight,
    conv_bias,
    skip_gain,
    query_heads,
    key_heads,
    value_heads,
):
    rows, channels = mixer_input.shape
    size = lax.axis_size("ctx")
    own = lax.axis_index("ctx")
    groups = channels // WIDE
    tiles = channels // LANES
    f32, bf16 = jnp.float32, jnp.bfloat16
    shape = jax.ShapeDtypeStruct

    rim = lax.ppermute(
        mixer_input[rows - (TAPS - 1) :], "ctx", [(i, i + 1) for i in range(size - 1)]
    )
    pairs = lax.all_gather(
        jnp.concatenate([key_heads, value_heads], axis=1), "ctx", axis=0, tiled=True
    )
    rates = -LOG2E * jnp.exp(decay_log)
    rates = rates.reshape(tiles, LANES, STATE).transpose(0, 2, 1).reshape(tiles * STATE, LANES)
    bc_rows = jnp.broadcast_to(
        jnp.concatenate([input_proj, output_proj], axis=0).reshape(-1, 1),
        (2 * rows * STATE, LANES),
    )
    b_spec = pl.BlockSpec((rows * STATE, LANES), lambda g: (0, 0))
    c_spec = pl.BlockSpec((rows * STATE, LANES), lambda g: (1, 0))
    share = tiles * STATE // size

    wide = pl.BlockSpec((rows, WIDE), lambda g: (0, g))
    slab = pl.BlockSpec((None, rows * SUB, LANES), lambda g: (g, 0, 0))
    rate_spec = pl.BlockSpec((SUB * STATE, LANES), lambda g: (g, 0))
    slab_shape = shape((groups, rows * SUB, LANES), f32)
    step, inner, entering = pl.pallas_call(
        first_pass,
        grid=(groups,),
        in_specs=[
            pl.BlockSpec((TAPS - 1, WIDE), lambda g: (0, g)),
            wide,
            wide,
            pl.BlockSpec((TAPS, WIDE), lambda g: (0, g)),
            pl.BlockSpec((1, WIDE), lambda g: (0, g)),
            rate_spec,
            b_spec,
            pl.BlockSpec((tiles * STATE, LANES), lambda g: (0, 0)),
        ],
        out_specs=[
            slab,
            slab,
            pl.BlockSpec((size, share, LANES), lambda g: (0, 0, 0)),
        ],
        out_shape=[
            slab_shape,
            slab_shape,
            shape((size, share, LANES), bf16),
        ],
        scratch_shapes=[
            pltpu.VMEM((SUB + rows, WIDE), f32),
            pltpu.VMEM((SUB * STATE, LANES), f32),
            pltpu.VMEM((size, HEAD + share, LANES), bf16),
            pltpu.VMEM((size, HEAD + share, LANES), bf16),
            pltpu.VMEM((size, share, LANES), bf16),
            pltpu.VMEM((size, share, LANES), bf16),
        ]
        + [pltpu.SemaphoreType.DMA((size,))] * 4,
        compiler_params=pltpu.CompilerParams(collective_id=0, has_side_effects=True),
        cost_estimate=pl.CostEstimate(
            flops=6 * rows * channels * STATE,
            bytes_accessed=8 * rows * channels,
            transcendentals=rows * channels * STATE,
        ),
        name="first_pass",
    )(rim, mixer_input, step_raw, conv_weight.T, conv_bias[None], rates, bc_rows, rates)

    entering = entering.reshape(tiles * STATE, LANES)
    panel = Q_HEADS // KV_HEADS * HEAD_DIM
    keys = rows * size
    attention = pl.pallas_call(
        attend,
        grid=(KV_HEADS,),
        in_specs=[
            pl.BlockSpec(memory_space=pltpu.SMEM),
            pl.BlockSpec((rows, panel), lambda g: (0, g)),
            pl.BlockSpec((keys, HEAD_DIM), lambda g: (0, g)),
            pl.BlockSpec((keys, HEAD_DIM), lambda g: (0, KV_HEADS + g)),
        ],
        out_specs=pl.BlockSpec((rows, panel), lambda g: (0, g)),
        out_shape=shape((rows, Q_HEADS * HEAD_DIM), bf16),
        cost_estimate=pl.CostEstimate(
            flops=4 * rows * Q_HEADS * keys * HEAD_DIM,
            bytes_accessed=4 * keys * KV_HEADS * HEAD_DIM,
            transcendentals=rows * Q_HEADS * keys,
        ),
        name="attend",
    )((own * rows).astype(jnp.int32)[None], query_heads, pairs, pairs)

    mixer_output = pl.pallas_call(
        second_pass,
        grid=(groups,),
        in_specs=[
            slab,
            slab,
            wide,
            pl.BlockSpec((SUB, LANES), lambda g: (g, 0)),
            rate_spec,
            b_spec,
            c_spec,
            rate_spec,
        ],
        out_specs=wide,
        out_shape=shape((rows, channels), bf16),
        scratch_shapes=[
            pltpu.VMEM((SUB * STATE, LANES), f32),
            pltpu.VMEM((rows * SUB, LANES), f32),
        ],
        cost_estimate=pl.CostEstimate(
            flops=8 * rows * channels * STATE,
            bytes_accessed=12 * rows * channels,
            transcendentals=rows * channels * STATE,
        ),
        name="second_pass",
    )(step, inner, gate_input, skip_gain.reshape(tiles, LANES), rates, bc_rows, bc_rows, entering)
    return (mixer_output, attention)


def solution(mesh):
    tokens = P(("groups", "ctx"), None)
    in_specs = (tokens,) * 5 + (P(),) * 4 + (tokens,) * 3
    return jax.shard_map(
        per_device, mesh=mesh, in_specs=in_specs, out_specs=(tokens, tokens), check_vma=False
    )
```

```python
import math

import jax
import jax.numpy as jnp
import numpy as np
from jax import lax
from jax.experimental import pallas as pl
from jax.experimental.pallas import tpu as pltpu
from jax.sharding import PartitionSpec as P

STATE = 16
TAPS = 4
Q_HEADS = 32
KV_HEADS = 4
HEAD_DIM = 128
LANES = 128
SUB = 8
WIDE = SUB * LANES
HEAD = 16
LOG2E = math.log2(math.e)


def silu(v):
    return v / (1.0 + jnp.exp(-v))


def first_pass(
    rim_ref, x_ref, raw_ref, w_ref, bias_ref, rate_ref, b_ref, all_rates_ref,
    key_ref, value_ref, step_ref, inner_ref, ent_ref, pairs_ref,
    ext, fin, snd, got, ans, lands, send_a, recv_a, send_b, recv_b, send_k, recv_k, own_k
):
    size, share, _ = ans.shape
    group = pl.program_id(0)
    groups = pl.num_programs(0)
    share_count = STATE * SUB // share
    count = max(1, SUB // share_count)
    per = share // count
    me = lax.axis_index("ctx")
    barrier = pltpu.get_barrier_semaphore()

    def greet(off, _):
        pl.semaphore_signal(
            barrier,
            inc=1,
            device_id={"ctx": lax.rem(me + off, size)},
            device_id_type=pl.DeviceIdType.MESH,
        )
        return 0

    stages = size.bit_length() - 1
    slot = sum(((me // 2**b) % 2) * 2 ** (stages - 1 - b) for b in range(stages))

    def own_copies():
        width = key_ref.shape[1]
        return [
            pltpu.make_async_copy(
                source, pairs_ref.at[slot, :, pl.ds(i * width, width)], own_k.at[i]
            )
            for i, source in enumerate((key_ref, value_ref))
        ]

    def double(stage):
        far = size // 2 ** (stage + 1)
        block = pl.ds((slot // 2**stage) * 2**stage, 2**stage)
        return pltpu.make_async_remote_copy(
            src_ref=pairs_ref.at[block],
            dst_ref=pairs_ref.at[block],
            send_sem=send_k.at[stage],
            recv_sem=recv_k.at[stage],
            device_id={"ctx": me + far - 2 * far * ((me // far) % 2)},
            device_id_type=pl.DeviceIdType.MESH,
        )

    @pl.when(group == 0)
    def _():
        lax.fori_loop(1, size, greet, 0)
        for copy in own_copies():
            copy.start()

    def ask(to, origin):
        return pltpu.make_async_remote_copy(
            src_ref=snd.at[to],
            dst_ref=got.at[origin],
            send_sem=send_a.at[to],
            recv_sem=recv_a.at[origin],
            device_id={"ctx": to},
            device_id_type=pl.DeviceIdType.MESH,
        )

    def answer(to, origin):
        return pltpu.make_async_remote_copy(
            src_ref=ans.at[to],
            dst_ref=lands.at[origin],
            send_sem=send_b.at[to],
            recv_sem=recv_b.at[origin],
            device_id={"ctx": to},
            device_id_type=pl.DeviceIdType.MESH,
        )

    rows = x_ref.shape[0]
    rim_rows = TAPS - 1
    ext[pl.ds(SUB - rim_rows, rim_rows), :] = rim_ref[...].astype(jnp.float32)
    ext[pl.ds(SUB, rows), :] = x_ref[...].astype(jnp.float32)
    for k in range(SUB):
        cols = pl.ds(k * LANES, LANES)
        conv = jnp.zeros((rows, LANES), jnp.float32) + bias_ref[:, cols]
        for tap in range(TAPS):
            conv = conv + w_ref[pl.ds(tap, 1), cols] * ext[pl.ds(SUB - rim_rows + tap, rows), cols]
        raw = raw_ref[:, cols].astype(jnp.float32)
        inner_ref[pl.ds(k, rows, stride=SUB), :] = silu(conv)
        step_ref[pl.ds(k, rows, stride=SUB), :] = jnp.maximum(raw, 0.0) + jnp.log1p(
            jnp.exp(-jnp.abs(raw))
        )
    rates = [rate_ref[pl.ds(n, SUB, stride=STATE), :] for n in range(STATE)]

    def one(t, carry):
        total, hs = carry
        step = step_ref[pl.ds(pl.multiple_of(t * SUB, SUB), SUB), :]
        u = step * inner_ref[pl.ds(pl.multiple_of(t * SUB, SUB), SUB), :]
        new = []
        for n in range(STATE):
            b = jnp.broadcast_to(b_ref[pl.ds(t * STATE + n, 1), :], (SUB, LANES))
            new.append(jnp.exp2(step * rates[n]) * hs[n] + u * b)
        return total + step, tuple(new)

    zero = jnp.zeros((SUB, LANES), jnp.float32)
    total, hs = lax.fori_loop(0, rows, one, (zero, (zero,) * STATE), unroll=2)
    for n in range(STATE):
        fin[pl.ds(n, SUB, stride=STATE), :] = hs[n]

    @pl.when(group == 0)
    def _():
        pl.semaphore_wait(barrier, size - 1)
        for copy in own_copies():
            copy.wait()
        double(0).start()

    for stage in range(2):

        @pl.when(group == 3 * stage + 3)
        def _():
            double(stage).wait()
            double(stage + 1).start()

    filler = jnp.zeros((HEAD - 3 * count, LANES), jnp.float32)
    for part in range(share_count):
        to = group * share_count + part
        first = part * SUB // share_count
        left = total[first : first + count]
        pieces = []
        for _ in range(3):
            pieces.append(left.astype(jnp.bfloat16).astype(jnp.float32))
            left = left - pieces[-1]
        snd[to, pl.ds(0, HEAD), :] = jnp.concatenate(pieces + [filler], axis=0).astype(jnp.bfloat16)
        snd[to, pl.ds(HEAD, share), :] = fin[pl.ds(part * share, share), :].astype(jnp.bfloat16)

        @pl.when(to != me)
        def _():
            ask(to, me).start()

    def join(d, hs):
        @pl.when(d != me)
        def _():
            ask(d, d).wait_recv()

        parts = got[d, pl.ds(0, HEAD), :].astype(jnp.float32)
        new = []
        for k in range(count):
            ans[d, pl.ds(k * per, per), :] = hs[k].astype(jnp.bfloat16)
            total = (
                parts[k : k + 1] + parts[count + k : count + k + 1]
            ) + parts[2 * count + k : 2 * count + k + 1]
            rate = all_rates_ref[pl.ds(pl.multiple_of(me * share + k * per, SUB), per), :]
            own = got[d, pl.ds(HEAD + k * per, per), :].astype(jnp.float32)
            new.append(jnp.exp2(rate * total) * hs[k] + own)

        @pl.when(d != me)
        def _():
            answer(d, me).start()

        return tuple(new)

    @pl.when(group == jnp.minimum(me // share_count + 2, groups - 1))
    def _():
        got[me] = snd[me]
        lax.fori_loop(0, size, join, (jnp.zeros((per, LANES), jnp.float32),) * count)
        lands[me] = ans[me]

    def finish(off, _):
        other = lax.rem(me + off, size)
        answer(other, other).wait_recv()
        ask(other, other).wait_send()
        answer(other, other).wait_send()
        return 0

    @pl.when(group == groups - 1)
    def _():
        lax.fori_loop(1, size, finish, 0)
        ent_ref[...] = lands[...]
        for stage in range(2, stages):
            double(stage).wait()
            if stage + 1 < stages:
                double(stage + 1).start()


def second_pass(
    step_ref, inner_ref, gate_ref, skip_ref, rate_ref, b_ref, c_ref, ent_ref, out_ref, ent, ysc
):
    rows = gate_ref.shape[0]
    ent[...] = ent_ref[...].astype(jnp.float32)
    rates = [rate_ref[pl.ds(n, SUB, stride=STATE), :] for n in range(STATE)]
    start = tuple(ent[pl.ds(n, SUB, stride=STATE), :] for n in range(STATE))
    skip = skip_ref[...]

    def one(t, hs):
        at = pl.ds(pl.multiple_of(t * SUB, SUB), SUB)
        step = step_ref[at, :]
        inner = inner_ref[at, :]
        u = step * inner
        sums = [skip * inner, None]
        new = []
        for n in range(STATE):
            row = pl.ds(t * STATE + n, 1)
            b = jnp.broadcast_to(b_ref[row, :], (SUB, LANES))
            c = jnp.broadcast_to(c_ref[row, :], (SUB, LANES))
            h = jnp.exp2(step * rates[n]) * hs[n] + u * b
            new.append(h)
            term = h * c
            sums[n % 2] = term if sums[n % 2] is None else sums[n % 2] + term
        ysc[at, :] = sums[0] + sums[1]
        return tuple(new)

    lax.fori_loop(0, rows, one, start, unroll=2)
    for k in range(SUB):
        cols = pl.ds(k * LANES, LANES)
        y = ysc[pl.ds(k, rows, stride=SUB), :]
        out_ref[:, cols] = (y * silu(gate_ref[:, cols].astype(jnp.float32))).astype(jnp.bfloat16)


def attend(place_ref, at_ref, q_ref, k_ref, v_ref, out_ref):
    rows = q_ref.shape[0]
    keys = k_ref.shape[0]
    heads = q_ref.shape[1] // HEAD_DIM
    chunk = math.gcd(keys, 1024)
    scale = LOG2E / math.sqrt(HEAD_DIM)
    q = jnp.concatenate([q_ref[:, pl.ds(h * HEAD_DIM, HEAD_DIM)] for h in range(heads)], axis=0)

    def fold(first, running):
        at = pl.ds(first, chunk)
        scores = lax.dot_general(
            q, k_ref[at, :], (((1,), (1,)), ((), ())), preferred_element_type=jnp.float32
        ).reshape(heads, rows, chunk)
        place = place_ref[0] + lax.broadcasted_iota(jnp.int32, (1, rows, chunk), 1)
        allowed = at_ref[:, at].reshape(1, 1, chunk) <= place
        scores = jnp.where(allowed, scores, -1e30)
        largest = jnp.max(scores, axis=2, keepdims=True)
        if running is not None:
            largest = jnp.maximum(largest, running[0])
        probs = jnp.exp2((scores - largest) * scale)
        totals = jnp.sum(probs, axis=2, keepdims=True)
        summed = jnp.dot(
            probs.reshape(heads * rows, chunk).astype(jnp.bfloat16),
            v_ref[at, :],
            preferred_element_type=jnp.float32,
        ).reshape(heads, rows, HEAD_DIM)
        if running is not None:
            shrink = jnp.exp2((running[0] - largest) * scale)
            totals = totals + running[1] * shrink
            summed = summed + running[2] * shrink
        return largest, totals, summed

    running = fold(0, None)
    if keys > chunk:
        running = lax.fori_loop(
            1,
            keys // chunk,
            lambda i, held: fold(pl.multiple_of(i * chunk, chunk), held),
            running,
        )
    out = (running[2] / running[1]).astype(jnp.bfloat16)
    for h in range(heads):
        out_ref[:, pl.ds(h * HEAD_DIM, HEAD_DIM)] = out[h]


def per_device(
    mixer_input,
    gate_input,
    step_raw,
    input_proj,
    output_proj,
    decay_log,
    conv_weight,
    conv_bias,
    skip_gain,
    query_heads,
    key_heads,
    value_heads,
):
    rows, channels = mixer_input.shape
    size = lax.axis_size("ctx")
    own = lax.axis_index("ctx")
    groups = channels // WIDE
    stages = size.bit_length() - 1
    tiles = channels // LANES
    f32, bf16 = jnp.float32, jnp.bfloat16
    shape = jax.ShapeDtypeStruct

    rim = lax.ppermute(
        mixer_input[rows - (TAPS - 1) :], "ctx", [(i, i + 1) for i in range(size - 1)]
    )
    rates = -LOG2E * jnp.exp(decay_log)
    rates = rates.reshape(tiles, LANES, STATE).transpose(0, 2, 1).reshape(tiles * STATE, LANES)
    bc_rows = jnp.broadcast_to(
        jnp.concatenate([input_proj, output_proj], axis=0).reshape(-1, 1),
        (2 * rows * STATE, LANES),
    )
    b_spec = pl.BlockSpec((rows * STATE, LANES), lambda g: (0, 0))
    c_spec = pl.BlockSpec((rows * STATE, LANES), lambda g: (1, 0))
    share = tiles * STATE // size

    wide = pl.BlockSpec((rows, WIDE), lambda g: (0, g))
    slab = pl.BlockSpec((None, rows * SUB, LANES), lambda g: (g, 0, 0))
    rate_spec = pl.BlockSpec((SUB * STATE, LANES), lambda g: (g, 0))
    slab_shape = shape((groups, rows * SUB, LANES), f32)
    step, inner, entering, pairs = pl.pallas_call(
        first_pass,
        grid=(groups,),
        in_specs=[
            pl.BlockSpec((TAPS - 1, WIDE), lambda g: (0, g)),
            wide,
            wide,
            pl.BlockSpec((TAPS, WIDE), lambda g: (0, g)),
            pl.BlockSpec((1, WIDE), lambda g: (0, g)),
            rate_spec,
            b_spec,
            pl.BlockSpec((tiles * STATE, LANES), lambda g: (0, 0)),
            pl.BlockSpec(memory_space=pl.ANY),
            pl.BlockSpec(memory_space=pl.ANY),
        ],
        out_specs=[
            slab,
            slab,
            pl.BlockSpec((size, share, LANES), lambda g: (0, 0, 0)),
            pl.BlockSpec(memory_space=pl.ANY),
        ],
        out_shape=[
            slab_shape,
            slab_shape,
            shape((size, share, LANES), bf16),
            shape((size, rows, 2 * KV_HEADS * HEAD_DIM), bf16),
        ],
        scratch_shapes=[
            pltpu.VMEM((SUB + rows, WIDE), f32),
            pltpu.VMEM((SUB * STATE, LANES), f32),
            pltpu.VMEM((size, HEAD + share, LANES), bf16),
            pltpu.VMEM((size, HEAD + share, LANES), bf16),
            pltpu.VMEM((size, share, LANES), bf16),
            pltpu.VMEM((size, share, LANES), bf16),
        ]
        + [pltpu.SemaphoreType.DMA((size,))] * 4
        + [pltpu.SemaphoreType.DMA((stages,))] * 2
        + [pltpu.SemaphoreType.DMA((2,))],
        compiler_params=pltpu.CompilerParams(collective_id=0, has_side_effects=True),
        cost_estimate=pl.CostEstimate(
            flops=6 * rows * channels * STATE,
            bytes_accessed=8 * rows * channels,
            transcendentals=rows * channels * STATE,
        ),
        name="first_pass",
    )(rim, mixer_input, step_raw, conv_weight.T, conv_bias[None], rates, bc_rows, rates, key_heads, value_heads)

    entering = entering.reshape(tiles * STATE, LANES)
    panel = Q_HEADS // KV_HEADS * HEAD_DIM
    keys = rows * size
    pairs = pairs.reshape(keys, 2 * KV_HEADS * HEAD_DIM)
    origin = [int(f"{p:0{stages}b}"[::-1], 2) for p in range(size)]
    key_places = jnp.asarray(
        (np.array(origin)[:, None] * rows + np.arange(rows)).reshape(1, keys), jnp.int32
    )
    attention = pl.pallas_call(
        attend,
        grid=(KV_HEADS,),
        in_specs=[
            pl.BlockSpec(memory_space=pltpu.SMEM),
            pl.BlockSpec((1, keys), lambda g: (0, 0)),
            pl.BlockSpec((rows, panel), lambda g: (0, g)),
            pl.BlockSpec((keys, HEAD_DIM), lambda g: (0, g)),
            pl.BlockSpec((keys, HEAD_DIM), lambda g: (0, KV_HEADS + g)),
        ],
        out_specs=pl.BlockSpec((rows, panel), lambda g: (0, g)),
        out_shape=shape((rows, Q_HEADS * HEAD_DIM), bf16),
        cost_estimate=pl.CostEstimate(
            flops=4 * rows * Q_HEADS * keys * HEAD_DIM,
            bytes_accessed=4 * keys * KV_HEADS * HEAD_DIM,
            transcendentals=rows * Q_HEADS * keys,
        ),
        name="attend",
    )((own * rows).astype(jnp.int32)[None], key_places, query_heads, pairs, pairs)

    mixer_output = pl.pallas_call(
        second_pass,
        grid=(groups,),
        in_specs=[
            slab,
            slab,
            wide,
            pl.BlockSpec((SUB, LANES), lambda g: (g, 0)),
            rate_spec,
            b_spec,
            c_spec,
            rate_spec,
        ],
        out_specs=wide,
        out_shape=shape((rows, channels), bf16),
        scratch_shapes=[
            pltpu.VMEM((SUB * STATE, LANES), f32),
            pltpu.VMEM((rows * SUB, LANES), f32),
        ],
        cost_estimate=pl.CostEstimate(
            flops=8 * rows * channels * STATE,
            bytes_accessed=12 * rows * channels,
            transcendentals=rows * channels * STATE,
        ),
        name="second_pass",
    )(step, inner, gate_input, skip_gain.reshape(tiles, LANES), rates, bc_rows, bc_rows, entering)
    return (mixer_output, attention)


def solution(mesh):
    tokens = P(("groups", "ctx"), None)
    in_specs = (tokens,) * 5 + (P(),) * 4 + (tokens,) * 3
    return jax.shard_map(
        per_device, mesh=mesh, in_specs=in_specs, out_specs=(tokens, tokens), check_vma=False
    )
```

```python
import math

import jax
import jax.numpy as jnp
import numpy as np
from jax import lax
from jax.experimental import pallas as pl
from jax.experimental.pallas import tpu as pltpu
from jax.sharding import PartitionSpec as P

STATE = 16
TAPS = 4
Q_HEADS = 32
KV_HEADS = 4
HEAD_DIM = 128
LANES = 128
SUB = 8
WIDE = SUB * LANES
HEAD = 16
LOG2E = math.log2(math.e)


def silu(v):
    return v / (1.0 + jnp.exp(-v))


EARLY = 2


def slot_of(size, me):
    stages = size.bit_length() - 1
    return sum(((me // 2**b) % 2) * 2 ** (stages - 1 - b) for b in range(stages)), stages


def partner(size, stage):
    me = lax.axis_index("ctx")
    far = size // 2 ** (stage + 1)
    return me + far - 2 * far * ((me // far) % 2)


def held(size, stage):
    slot, _ = slot_of(size, lax.axis_index("ctx"))
    return pl.ds((slot // 2**stage) * 2**stage, 2**stage)


def doubling(size, stage, source, target, send, recv):
    return pltpu.make_async_remote_copy(
        src_ref=source.at[held(size, stage)],
        dst_ref=target.at[held(size, stage)],
        send_sem=send.at[stage],
        recv_sem=recv.at[stage],
        device_id={"ctx": partner(size, stage)},
        device_id_type=pl.DeviceIdType.MESH,
    )


def first_pass(
    rim_ref, x_ref, raw_ref, w_ref, bias_ref, rate_ref, b_ref, all_rates_ref,
    key_ref, value_ref, step_ref, inner_ref, ent_ref, pairs_ref,
    ext, fin, snd, got, ans, lands, send_a, recv_a, send_b, recv_b, send_k, recv_k, own_k
):
    size, share, _ = ans.shape
    group = pl.program_id(0)
    groups = pl.num_programs(0)
    share_count = STATE * SUB // share
    count = max(1, SUB // share_count)
    per = share // count
    me = lax.axis_index("ctx")
    barrier = pltpu.get_barrier_semaphore()

    def greet(off, _):
        pl.semaphore_signal(
            barrier,
            inc=1,
            device_id={"ctx": lax.rem(me + off, size)},
            device_id_type=pl.DeviceIdType.MESH,
        )
        return 0

    slot, _ = slot_of(size, me)

    def own_copies():
        width = key_ref.shape[1]
        return [
            pltpu.make_async_copy(
                source, pairs_ref.at[slot, :, pl.ds(i * width, width)], own_k.at[i]
            )
            for i, source in enumerate((key_ref, value_ref))
        ]

    def double(stage):
        return doubling(size, stage, pairs_ref, pairs_ref, send_k, recv_k)

    @pl.when(group == 0)
    def _():
        lax.fori_loop(1, size, greet, 0)
        for copy in own_copies():
            copy.start()

    def ask(to, origin):
        return pltpu.make_async_remote_copy(
            src_ref=snd.at[to],
            dst_ref=got.at[origin],
            send_sem=send_a.at[to],
            recv_sem=recv_a.at[origin],
            device_id={"ctx": to},
            device_id_type=pl.DeviceIdType.MESH,
        )

    def answer(to, origin):
        return pltpu.make_async_remote_copy(
            src_ref=ans.at[to],
            dst_ref=lands.at[origin],
            send_sem=send_b.at[to],
            recv_sem=recv_b.at[origin],
            device_id={"ctx": to},
            device_id_type=pl.DeviceIdType.MESH,
        )

    rows = x_ref.shape[0]
    rim_rows = TAPS - 1
    ext[pl.ds(SUB - rim_rows, rim_rows), :] = rim_ref[...].astype(jnp.float32)
    ext[pl.ds(SUB, rows), :] = x_ref[...].astype(jnp.float32)
    for k in range(SUB):
        cols = pl.ds(k * LANES, LANES)
        conv = jnp.zeros((rows, LANES), jnp.float32) + bias_ref[:, cols]
        for tap in range(TAPS):
            conv = conv + w_ref[pl.ds(tap, 1), cols] * ext[pl.ds(SUB - rim_rows + tap, rows), cols]
        raw = raw_ref[:, cols].astype(jnp.float32)
        inner_ref[pl.ds(k, rows, stride=SUB), :] = silu(conv)
        step_ref[pl.ds(k, rows, stride=SUB), :] = jnp.maximum(raw, 0.0) + jnp.log1p(
            jnp.exp(-jnp.abs(raw))
        )
    rates = [rate_ref[pl.ds(n, SUB, stride=STATE), :] for n in range(STATE)]

    def one(t, carry):
        total, hs = carry
        step = step_ref[pl.ds(pl.multiple_of(t * SUB, SUB), SUB), :]
        u = step * inner_ref[pl.ds(pl.multiple_of(t * SUB, SUB), SUB), :]
        new = []
        for n in range(STATE):
            b = jnp.broadcast_to(b_ref[pl.ds(t * STATE + n, 1), :], (SUB, LANES))
            new.append(jnp.exp2(step * rates[n]) * hs[n] + u * b)
        return total + step, tuple(new)

    zero = jnp.zeros((SUB, LANES), jnp.float32)
    total, hs = lax.fori_loop(0, rows, one, (zero, (zero,) * STATE), unroll=2)
    for n in range(STATE):
        fin[pl.ds(n, SUB, stride=STATE), :] = hs[n]

    @pl.when(group == 0)
    def _():
        pl.semaphore_wait(barrier, size - 1)
        for copy in own_copies():
            copy.wait()
        double(0).start()

    @pl.when(group == 5)
    def _():
        double(0).wait()
        double(1).start()

    filler = jnp.zeros((HEAD - 3 * count, LANES), jnp.float32)
    for part in range(share_count):
        to = group * share_count + part
        first = part * SUB // share_count
        left = total[first : first + count]
        pieces = []
        for _ in range(3):
            pieces.append(left.astype(jnp.bfloat16).astype(jnp.float32))
            left = left - pieces[-1]
        snd[to, pl.ds(0, HEAD), :] = jnp.concatenate(pieces + [filler], axis=0).astype(jnp.bfloat16)
        snd[to, pl.ds(HEAD, share), :] = fin[pl.ds(part * share, share), :].astype(jnp.bfloat16)

        @pl.when(to != me)
        def _():
            ask(to, me).start()

    def join(d, hs):
        @pl.when(d != me)
        def _():
            ask(d, d).wait_recv()

        parts = got[d, pl.ds(0, HEAD), :].astype(jnp.float32)
        new = []
        for k in range(count):
            ans[d, pl.ds(k * per, per), :] = hs[k].astype(jnp.bfloat16)
            total = (
                parts[k : k + 1] + parts[count + k : count + k + 1]
            ) + parts[2 * count + k : 2 * count + k + 1]
            rate = all_rates_ref[pl.ds(pl.multiple_of(me * share + k * per, SUB), per), :]
            own = got[d, pl.ds(HEAD + k * per, per), :].astype(jnp.float32)
            new.append(jnp.exp2(rate * total) * hs[k] + own)

        @pl.when(d != me)
        def _():
            answer(d, me).start()

        return tuple(new)

    @pl.when(group == jnp.minimum(me // share_count + 2, groups - 1))
    def _():
        got[me] = snd[me]
        lax.fori_loop(0, size, join, (jnp.zeros((per, LANES), jnp.float32),) * count)
        lands[me] = ans[me]

    def finish(off, _):
        other = lax.rem(me + off, size)
        answer(other, other).wait_recv()
        ask(other, other).wait_send()
        answer(other, other).wait_send()
        return 0

    @pl.when(group == groups - 1)
    def _():
        lax.fori_loop(1, size, finish, 0)
        ent_ref[...] = lands[...]
        double(1).wait()


def second_pass(
    step_ref, inner_ref, gate_ref, skip_ref, rate_ref, b_ref, c_ref, ent_ref, some_ref,
    out_ref, pairs_ref, ent, ysc, send_k, recv_k, own_k
):
    rows = gate_ref.shape[0]
    size = some_ref.shape[0]
    group = pl.program_id(0)
    groups = pl.num_programs(0)
    stages = size.bit_length() - 1
    barrier = pltpu.get_barrier_semaphore()

    def carry_over():
        block = held(size, EARLY)
        return pltpu.make_async_copy(some_ref.at[block], pairs_ref.at[block], own_k.at[0])

    def double(stage):
        source = some_ref if stage == EARLY else pairs_ref
        return doubling(size, stage, source, pairs_ref, send_k, recv_k)

    @pl.when(group == 0)
    def _():
        for stage in range(EARLY, stages):
            pl.semaphore_signal(
                barrier,
                inc=1,
                device_id={"ctx": partner(size, stage)},
                device_id_type=pl.DeviceIdType.MESH,
            )
        carry_over().start()
        pl.semaphore_wait(barrier, stages - EARLY)
        double(EARLY).start()

    ent[...] = ent_ref[...].astype(jnp.float32)
    rates = [rate_ref[pl.ds(n, SUB, stride=STATE), :] for n in range(STATE)]
    start = tuple(ent[pl.ds(n, SUB, stride=STATE), :] for n in range(STATE))
    skip = skip_ref[...]

    def one(t, hs):
        at = pl.ds(pl.multiple_of(t * SUB, SUB), SUB)
        step = step_ref[at, :]
        inner = inner_ref[at, :]
        u = step * inner
        sums = [skip * inner, None]
        new = []
        for n in range(STATE):
            row = pl.ds(t * STATE + n, 1)
            b = jnp.broadcast_to(b_ref[row, :], (SUB, LANES))
            c = jnp.broadcast_to(c_ref[row, :], (SUB, LANES))
            h = jnp.exp2(step * rates[n]) * hs[n] + u * b
            new.append(h)
            term = h * c
            sums[n % 2] = term if sums[n % 2] is None else sums[n % 2] + term
        ysc[at, :] = sums[0] + sums[1]
        return tuple(new)

    lax.fori_loop(0, rows, one, start, unroll=2)
    for k in range(SUB):
        cols = pl.ds(k * LANES, LANES)
        y = ysc[pl.ds(k, rows, stride=SUB), :]
        out_ref[:, cols] = (y * silu(gate_ref[:, cols].astype(jnp.float32))).astype(jnp.bfloat16)

    @pl.when(group == groups - 2)
    def _():
        carry_over().wait()
        double(EARLY).wait()
        double(EARLY + 1).start()

    @pl.when(group == groups - 1)
    def _():
        for stage in range(EARLY + 1, stages):
            double(stage).wait()
            if stage + 1 < stages:
                double(stage + 1).start()


def attend(place_ref, at_ref, q_ref, k_ref, v_ref, out_ref):
    rows = q_ref.shape[0]
    keys = k_ref.shape[0]
    heads = q_ref.shape[1] // HEAD_DIM
    chunk = math.gcd(keys, 1024)
    scale = LOG2E / math.sqrt(HEAD_DIM)
    q = jnp.concatenate([q_ref[:, pl.ds(h * HEAD_DIM, HEAD_DIM)] for h in range(heads)], axis=0)

    def fold(first, running):
        at = pl.ds(first, chunk)
        scores = lax.dot_general(
            q, k_ref[at, :], (((1,), (1,)), ((), ())), preferred_element_type=jnp.float32
        ).reshape(heads, rows, chunk)
        place = place_ref[0] + lax.broadcasted_iota(jnp.int32, (1, rows, chunk), 1)
        allowed = at_ref[:, at].reshape(1, 1, chunk) <= place
        scores = jnp.where(allowed, scores, -1e30)
        largest = jnp.max(scores, axis=2, keepdims=True)
        if running is not None:
            largest = jnp.maximum(largest, running[0])
        probs = jnp.exp2((scores - largest) * scale)
        totals = jnp.sum(probs, axis=2, keepdims=True)
        summed = jnp.dot(
            probs.reshape(heads * rows, chunk).astype(jnp.bfloat16),
            v_ref[at, :],
            preferred_element_type=jnp.float32,
        ).reshape(heads, rows, HEAD_DIM)
        if running is not None:
            shrink = jnp.exp2((running[0] - largest) * scale)
            totals = totals + running[1] * shrink
            summed = summed + running[2] * shrink
        return largest, totals, summed

    running = fold(0, None)
    if keys > chunk:
        running = lax.fori_loop(
            1,
            keys // chunk,
            lambda i, held: fold(pl.multiple_of(i * chunk, chunk), held),
            running,
        )
    out = (running[2] / running[1]).astype(jnp.bfloat16)
    for h in range(heads):
        out_ref[:, pl.ds(h * HEAD_DIM, HEAD_DIM)] = out[h]


def per_device(
    mixer_input,
    gate_input,
    step_raw,
    input_proj,
    output_proj,
    decay_log,
    conv_weight,
    conv_bias,
    skip_gain,
    query_heads,
    key_heads,
    value_heads,
):
    rows, channels = mixer_input.shape
    size = lax.axis_size("ctx")
    own = lax.axis_index("ctx")
    groups = channels // WIDE
    stages = size.bit_length() - 1
    tiles = channels // LANES
    f32, bf16 = jnp.float32, jnp.bfloat16
    shape = jax.ShapeDtypeStruct

    rim = lax.ppermute(
        mixer_input[rows - (TAPS - 1) :], "ctx", [(i, i + 1) for i in range(size - 1)]
    )
    rates = -LOG2E * jnp.exp(decay_log)
    rates = rates.reshape(tiles, LANES, STATE).transpose(0, 2, 1).reshape(tiles * STATE, LANES)
    bc_rows = jnp.broadcast_to(
        jnp.concatenate([input_proj, output_proj], axis=0).reshape(-1, 1),
        (2 * rows * STATE, LANES),
    )
    b_spec = pl.BlockSpec((rows * STATE, LANES), lambda g: (0, 0))
    c_spec = pl.BlockSpec((rows * STATE, LANES), lambda g: (1, 0))
    share = tiles * STATE // size

    wide = pl.BlockSpec((rows, WIDE), lambda g: (0, g))
    slab = pl.BlockSpec((None, rows * SUB, LANES), lambda g: (g, 0, 0))
    rate_spec = pl.BlockSpec((SUB * STATE, LANES), lambda g: (g, 0))
    slab_shape = shape((groups, rows * SUB, LANES), f32)
    step, inner, entering, some = pl.pallas_call(
        first_pass,
        grid=(groups,),
        in_specs=[
            pl.BlockSpec((TAPS - 1, WIDE), lambda g: (0, g)),
            wide,
            wide,
            pl.BlockSpec((TAPS, WIDE), lambda g: (0, g)),
            pl.BlockSpec((1, WIDE), lambda g: (0, g)),
            rate_spec,
            b_spec,
            pl.BlockSpec((tiles * STATE, LANES), lambda g: (0, 0)),
            pl.BlockSpec(memory_space=pl.ANY),
            pl.BlockSpec(memory_space=pl.ANY),
        ],
        out_specs=[
            slab,
            slab,
            pl.BlockSpec((size, share, LANES), lambda g: (0, 0, 0)),
            pl.BlockSpec(memory_space=pl.ANY),
        ],
        out_shape=[
            slab_shape,
            slab_shape,
            shape((size, share, LANES), bf16),
            shape((size, rows, 2 * KV_HEADS * HEAD_DIM), bf16),
        ],
        scratch_shapes=[
            pltpu.VMEM((SUB + rows, WIDE), f32),
            pltpu.VMEM((SUB * STATE, LANES), f32),
            pltpu.VMEM((size, HEAD + share, LANES), bf16),
            pltpu.VMEM((size, HEAD + share, LANES), bf16),
            pltpu.VMEM((size, share, LANES), bf16),
            pltpu.VMEM((size, share, LANES), bf16),
        ]
        + [pltpu.SemaphoreType.DMA((size,))] * 4
        + [pltpu.SemaphoreType.DMA((stages,))] * 2
        + [pltpu.SemaphoreType.DMA((2,))],
        compiler_params=pltpu.CompilerParams(collective_id=0, has_side_effects=True),
        cost_estimate=pl.CostEstimate(
            flops=6 * rows * channels * STATE,
            bytes_accessed=8 * rows * channels,
            transcendentals=rows * channels * STATE,
        ),
        name="first_pass",
    )(rim, mixer_input, step_raw, conv_weight.T, conv_bias[None], rates, bc_rows, rates, key_heads, value_heads)

    entering = entering.reshape(tiles * STATE, LANES)
    mixer_output, pairs = pl.pallas_call(
        second_pass,
        grid=(groups,),
        in_specs=[
            slab,
            slab,
            wide,
            pl.BlockSpec((SUB, LANES), lambda g: (g, 0)),
            rate_spec,
            b_spec,
            c_spec,
            rate_spec,
            pl.BlockSpec(memory_space=pl.ANY),
        ],
        out_specs=[wide, pl.BlockSpec(memory_space=pl.ANY)],
        out_shape=[
            shape((rows, channels), bf16),
            shape((size, rows, 2 * KV_HEADS * HEAD_DIM), bf16),
        ],
        scratch_shapes=[
            pltpu.VMEM((SUB * STATE, LANES), f32),
            pltpu.VMEM((rows * SUB, LANES), f32),
        ]
        + [pltpu.SemaphoreType.DMA((stages,))] * 2
        + [pltpu.SemaphoreType.DMA((1,))],
        compiler_params=pltpu.CompilerParams(collective_id=1, has_side_effects=True),
        cost_estimate=pl.CostEstimate(
            flops=8 * rows * channels * STATE,
            bytes_accessed=12 * rows * channels,
            transcendentals=rows * channels * STATE,
        ),
        name="second_pass",
    )(step, inner, gate_input, skip_gain.reshape(tiles, LANES), rates, bc_rows, bc_rows, entering, some)
    panel = Q_HEADS // KV_HEADS * HEAD_DIM
    keys = rows * size
    pairs = pairs.reshape(keys, 2 * KV_HEADS * HEAD_DIM)
    origin = [int(f"{p:0{stages}b}"[::-1], 2) for p in range(size)]
    key_places = jnp.asarray(
        (np.array(origin)[:, None] * rows + np.arange(rows)).reshape(1, keys), jnp.int32
    )
    attention = pl.pallas_call(
        attend,
        grid=(KV_HEADS,),
        in_specs=[
            pl.BlockSpec(memory_space=pltpu.SMEM),
            pl.BlockSpec((1, keys), lambda g: (0, 0)),
            pl.BlockSpec((rows, panel), lambda g: (0, g)),
            pl.BlockSpec((keys, HEAD_DIM), lambda g: (0, g)),
            pl.BlockSpec((keys, HEAD_DIM), lambda g: (0, KV_HEADS + g)),
        ],
        out_specs=pl.BlockSpec((rows, panel), lambda g: (0, g)),
        out_shape=shape((rows, Q_HEADS * HEAD_DIM), bf16),
        cost_estimate=pl.CostEstimate(
            flops=4 * rows * Q_HEADS * keys * HEAD_DIM,
            bytes_accessed=4 * keys * KV_HEADS * HEAD_DIM,
            transcendentals=rows * Q_HEADS * keys,
        ),
        name="attend",
    )((own * rows).astype(jnp.int32)[None], key_places, query_heads, pairs, pairs)

    return (mixer_output, attention)


def solution(mesh):
    tokens = P(("groups", "ctx"), None)
    in_specs = (tokens,) * 5 + (P(),) * 4 + (tokens,) * 3
    return jax.shard_map(
        per_device, mesh=mesh, in_specs=in_specs, out_specs=(tokens, tokens), check_vma=False
    )
```

```python
import math

import jax
import jax.numpy as jnp
import numpy as np
from jax import lax
from jax.experimental import pallas as pl
from jax.experimental.pallas import tpu as pltpu
from jax.sharding import PartitionSpec as P

STATE = 16
TAPS = 4
Q_HEADS = 32
KV_HEADS = 4
HEAD_DIM = 128
LANES = 128
SUB = 8
WIDE = SUB * LANES
HEAD = 16
LOG2E = math.log2(math.e)


def silu(v):
    return v / (1.0 + jnp.exp(-v))


EARLY = 2


def slot_of(size, me):
    stages = size.bit_length() - 1
    return sum(((me // 2**b) % 2) * 2 ** (stages - 1 - b) for b in range(stages)), stages


def partner(size, stage):
    me = lax.axis_index("ctx")
    far = size // 2 ** (stage + 1)
    return me + far - 2 * far * ((me // far) % 2)


def held(size, stage):
    slot, _ = slot_of(size, lax.axis_index("ctx"))
    return pl.ds((slot // 2**stage) * 2**stage, 2**stage)


def doubling(size, stage, source, target, send, recv):
    return pltpu.make_async_remote_copy(
        src_ref=source.at[held(size, stage)],
        dst_ref=target.at[held(size, stage)],
        send_sem=send.at[stage],
        recv_sem=recv.at[stage],
        device_id={"ctx": partner(size, stage)},
        device_id_type=pl.DeviceIdType.MESH,
    )


def first_pass(
    rim_ref, x_ref, raw_ref, w_ref, bias_ref, rate_ref, b_ref, all_rates_ref,
    key_ref, value_ref, step_ref, inner_ref, ent_ref, pairs_ref,
    ext, fin, snd, got, ans, lands, send_a, recv_a, send_b, recv_b, send_k, recv_k, own_k
):
    size, share, _ = ans.shape
    group = pl.program_id(0)
    groups = pl.num_programs(0)
    share_count = STATE * SUB // share
    count = max(1, SUB // share_count)
    per = share // count
    me = lax.axis_index("ctx")
    barrier = pltpu.get_barrier_semaphore()

    def greet(off, _):
        pl.semaphore_signal(
            barrier,
            inc=1,
            device_id={"ctx": lax.rem(me + off, size)},
            device_id_type=pl.DeviceIdType.MESH,
        )
        return 0

    slot, _ = slot_of(size, me)

    def own_copies():
        width = key_ref.shape[1]
        return [
            pltpu.make_async_copy(
                source, pairs_ref.at[slot, :, pl.ds(i * width, width)], own_k.at[i]
            )
            for i, source in enumerate((key_ref, value_ref))
        ]

    def double(stage):
        return doubling(size, stage, pairs_ref, pairs_ref, send_k, recv_k)

    @pl.when(group == 0)
    def _():
        lax.fori_loop(1, size, greet, 0)
        for copy in own_copies():
            copy.start()

    def ask(to, origin):
        return pltpu.make_async_remote_copy(
            src_ref=snd.at[to],
            dst_ref=got.at[origin],
            send_sem=send_a.at[to],
            recv_sem=recv_a.at[origin],
            device_id={"ctx": to},
            device_id_type=pl.DeviceIdType.MESH,
        )

    def answer(to, origin):
        return pltpu.make_async_remote_copy(
            src_ref=ans.at[to],
            dst_ref=lands.at[origin],
            send_sem=send_b.at[to],
            recv_sem=recv_b.at[origin],
            device_id={"ctx": to},
            device_id_type=pl.DeviceIdType.MESH,
        )

    rows = x_ref.shape[0]
    rim_rows = TAPS - 1
    ext[pl.ds(SUB - rim_rows, rim_rows), :] = rim_ref[...].astype(jnp.float32)
    ext[pl.ds(SUB, rows), :] = x_ref[...].astype(jnp.float32)
    for k in range(SUB):
        cols = pl.ds(k * LANES, LANES)
        conv = jnp.zeros((rows, LANES), jnp.float32) + bias_ref[:, cols]
        for tap in range(TAPS):
            conv = conv + w_ref[pl.ds(tap, 1), cols] * ext[pl.ds(SUB - rim_rows + tap, rows), cols]
        raw = raw_ref[:, cols].astype(jnp.float32)
        inner_ref[pl.ds(k, rows, stride=SUB), :] = silu(conv)
        step_ref[pl.ds(k, rows, stride=SUB), :] = jnp.maximum(raw, 0.0) + jnp.log1p(
            jnp.exp(-jnp.abs(raw))
        )
    rates = [rate_ref[pl.ds(n, SUB, stride=STATE), :] for n in range(STATE)]

    def one(t, carry):
        total, hs = carry
        step = step_ref[pl.ds(pl.multiple_of(t * SUB, SUB), SUB), :]
        u = step * inner_ref[pl.ds(pl.multiple_of(t * SUB, SUB), SUB), :]
        new = []
        for n in range(STATE):
            b = jnp.broadcast_to(b_ref[pl.ds(t * STATE + n, 1), :], (SUB, LANES))
            new.append(jnp.exp2(step * rates[n]) * hs[n] + u * b)
        return total + step, tuple(new)

    zero = jnp.zeros((SUB, LANES), jnp.float32)
    total, hs = lax.fori_loop(0, rows, one, (zero, (zero,) * STATE), unroll=2)
    for n in range(STATE):
        fin[pl.ds(n, SUB, stride=STATE), :] = hs[n]

    @pl.when(group == 0)
    def _():
        pl.semaphore_wait(barrier, size - 1)
        for copy in own_copies():
            copy.wait()
        double(0).start()

    @pl.when(group == groups - 1)
    def _():
        double(0).wait()
        double(1).start()

    filler = jnp.zeros((HEAD - 3 * count, LANES), jnp.float32)
    for part in range(share_count):
        to = group * share_count + part
        first = part * SUB // share_count
        left = total[first : first + count]
        pieces = []
        for _ in range(3):
            pieces.append(left.astype(jnp.bfloat16).astype(jnp.float32))
            left = left - pieces[-1]
        snd[to, pl.ds(0, HEAD), :] = jnp.concatenate(pieces + [filler], axis=0).astype(jnp.bfloat16)
        snd[to, pl.ds(HEAD, share), :] = fin[pl.ds(part * share, share), :].astype(jnp.bfloat16)

        @pl.when(to != me)
        def _():
            ask(to, me).start()

    def join(d, hs):
        @pl.when(d != me)
        def _():
            ask(d, d).wait_recv()

        parts = got[d, pl.ds(0, HEAD), :].astype(jnp.float32)
        new = []
        for k in range(count):
            ans[d, pl.ds(k * per, per), :] = hs[k].astype(jnp.bfloat16)
            total = (
                parts[k : k + 1] + parts[count + k : count + k + 1]
            ) + parts[2 * count + k : 2 * count + k + 1]
            rate = all_rates_ref[pl.ds(pl.multiple_of(me * share + k * per, SUB), per), :]
            own = got[d, pl.ds(HEAD + k * per, per), :].astype(jnp.float32)
            new.append(jnp.exp2(rate * total) * hs[k] + own)

        @pl.when(d != me)
        def _():
            answer(d, me).start()

        return tuple(new)

    @pl.when(group == groups - 1)
    def _():
        got[me] = snd[me]
        lax.fori_loop(0, size, join, (jnp.zeros((per, LANES), jnp.float32),) * count)
        lands[me] = ans[me]

    def finish(off, _):
        other = lax.rem(me + off, size)
        answer(other, other).wait_recv()
        ask(other, other).wait_send()
        answer(other, other).wait_send()
        return 0

    @pl.when(group == groups - 1)
    def _():
        lax.fori_loop(1, size, finish, 0)
        ent_ref[...] = lands[...]
        double(1).wait()


def second_pass(
    step_ref, inner_ref, gate_ref, skip_ref, rate_ref, b_ref, c_ref, ent_ref, some_ref,
    out_ref, pairs_ref, ent, ysc, send_k, recv_k, own_k
):
    rows = gate_ref.shape[0]
    size = some_ref.shape[0]
    group = pl.program_id(0)
    groups = pl.num_programs(0)
    stages = size.bit_length() - 1
    barrier = pltpu.get_barrier_semaphore()

    def carry_over():
        block = held(size, EARLY)
        return pltpu.make_async_copy(some_ref.at[block], pairs_ref.at[block], own_k.at[0])

    def double(stage):
        source = some_ref if stage == EARLY else pairs_ref
        return doubling(size, stage, source, pairs_ref, send_k, recv_k)

    @pl.when(group == 0)
    def _():
        for stage in range(EARLY, stages):
            pl.semaphore_signal(
                barrier,
                inc=1,
                device_id={"ctx": partner(size, stage)},
                device_id_type=pl.DeviceIdType.MESH,
            )
        carry_over().start()
        pl.semaphore_wait(barrier, stages - EARLY)
        double(EARLY).start()

    ent[...] = ent_ref[...].astype(jnp.float32)
    rates = [rate_ref[pl.ds(n, SUB, stride=STATE), :] for n in range(STATE)]
    start = tuple(ent[pl.ds(n, SUB, stride=STATE), :] for n in range(STATE))
    skip = skip_ref[...]

    def one(t, hs):
        at = pl.ds(pl.multiple_of(t * SUB, SUB), SUB)
        step = step_ref[at, :]
        inner = inner_ref[at, :]
        u = step * inner
        sums = [skip * inner, None]
        new = []
        for n in range(STATE):
            row = pl.ds(t * STATE + n, 1)
            b = jnp.broadcast_to(b_ref[row, :], (SUB, LANES))
            c = jnp.broadcast_to(c_ref[row, :], (SUB, LANES))
            h = jnp.exp2(step * rates[n]) * hs[n] + u * b
            new.append(h)
            term = h * c
            sums[n % 2] = term if sums[n % 2] is None else sums[n % 2] + term
        ysc[at, :] = sums[0] + sums[1]
        return tuple(new)

    lax.fori_loop(0, rows, one, start, unroll=2)
    for k in range(SUB):
        cols = pl.ds(k * LANES, LANES)
        y = ysc[pl.ds(k, rows, stride=SUB), :]
        out_ref[:, cols] = (y * silu(gate_ref[:, cols].astype(jnp.float32))).astype(jnp.bfloat16)

    @pl.when(group == groups - 2)
    def _():
        carry_over().wait()
        double(EARLY).wait()
        double(EARLY + 1).start()

    @pl.when(group == groups - 1)
    def _():
        for stage in range(EARLY + 1, stages):
            double(stage).wait()
            if stage + 1 < stages:
                double(stage + 1).start()


def attend(place_ref, at_ref, q_ref, k_ref, v_ref, out_ref):
    rows = q_ref.shape[0]
    keys = k_ref.shape[0]
    heads = q_ref.shape[1] // HEAD_DIM
    chunk = math.gcd(keys, 1024)
    scale = LOG2E / math.sqrt(HEAD_DIM)
    q = jnp.concatenate([q_ref[:, pl.ds(h * HEAD_DIM, HEAD_DIM)] for h in range(heads)], axis=0)

    def fold(first, running):
        at = pl.ds(first, chunk)
        scores = lax.dot_general(
            q, k_ref[at, :], (((1,), (1,)), ((), ())), preferred_element_type=jnp.float32
        ).reshape(heads, rows, chunk)
        place = place_ref[0] + lax.broadcasted_iota(jnp.int32, (1, rows, chunk), 1)
        allowed = at_ref[:, at].reshape(1, 1, chunk) <= place
        scores = jnp.where(allowed, scores, -1e30)
        largest = jnp.max(scores, axis=2, keepdims=True)
        if running is not None:
            largest = jnp.maximum(largest, running[0])
        probs = jnp.exp2((scores - largest) * scale)
        totals = jnp.sum(probs, axis=2, keepdims=True)
        summed = jnp.dot(
            probs.reshape(heads * rows, chunk).astype(jnp.bfloat16),
            v_ref[at, :],
            preferred_element_type=jnp.float32,
        ).reshape(heads, rows, HEAD_DIM)
        if running is not None:
            shrink = jnp.exp2((running[0] - largest) * scale)
            totals = totals + running[1] * shrink
            summed = summed + running[2] * shrink
        return largest, totals, summed

    running = fold(0, None)
    if keys > chunk:
        running = lax.fori_loop(
            1,
            keys // chunk,
            lambda i, held: fold(pl.multiple_of(i * chunk, chunk), held),
            running,
        )
    out = (running[2] / running[1]).astype(jnp.bfloat16)
    for h in range(heads):
        out_ref[:, pl.ds(h * HEAD_DIM, HEAD_DIM)] = out[h]


def per_device(
    mixer_input,
    gate_input,
    step_raw,
    input_proj,
    output_proj,
    decay_log,
    conv_weight,
    conv_bias,
    skip_gain,
    query_heads,
    key_heads,
    value_heads,
):
    rows, channels = mixer_input.shape
    size = lax.axis_size("ctx")
    own = lax.axis_index("ctx")
    groups = channels // WIDE
    stages = size.bit_length() - 1
    tiles = channels // LANES
    f32, bf16 = jnp.float32, jnp.bfloat16
    shape = jax.ShapeDtypeStruct

    rim = lax.ppermute(
        mixer_input[rows - (TAPS - 1) :], "ctx", [(i, i + 1) for i in range(size - 1)]
    )
    rates = -LOG2E * jnp.exp(decay_log)
    rates = rates.reshape(tiles, LANES, STATE).transpose(0, 2, 1).reshape(tiles * STATE, LANES)
    bc_rows = jnp.broadcast_to(
        jnp.concatenate([input_proj, output_proj], axis=0).reshape(-1, 1),
        (2 * rows * STATE, LANES),
    )
    b_spec = pl.BlockSpec((rows * STATE, LANES), lambda g: (0, 0))
    c_spec = pl.BlockSpec((rows * STATE, LANES), lambda g: (1, 0))
    share = tiles * STATE // size

    wide = pl.BlockSpec((rows, WIDE), lambda g: (0, g))
    slab = pl.BlockSpec((None, rows * SUB, LANES), lambda g: (g, 0, 0))
    rate_spec = pl.BlockSpec((SUB * STATE, LANES), lambda g: (g, 0))
    slab_shape = shape((groups, rows * SUB, LANES), f32)
    step, inner, entering, some = pl.pallas_call(
        first_pass,
        grid=(groups,),
        in_specs=[
            pl.BlockSpec((TAPS - 1, WIDE), lambda g: (0, g)),
            wide,
            wide,
            pl.BlockSpec((TAPS, WIDE), lambda g: (0, g)),
            pl.BlockSpec((1, WIDE), lambda g: (0, g)),
            rate_spec,
            b_spec,
            pl.BlockSpec((tiles * STATE, LANES), lambda g: (0, 0)),
            pl.BlockSpec(memory_space=pl.ANY),
            pl.BlockSpec(memory_space=pl.ANY),
        ],
        out_specs=[
            slab,
            slab,
            pl.BlockSpec((size, share, LANES), lambda g: (0, 0, 0)),
            pl.BlockSpec(memory_space=pl.ANY),
        ],
        out_shape=[
            slab_shape,
            slab_shape,
            shape((size, share, LANES), bf16),
            shape((size, rows, 2 * KV_HEADS * HEAD_DIM), bf16),
        ],
        scratch_shapes=[
            pltpu.VMEM((SUB + rows, WIDE), f32),
            pltpu.VMEM((SUB * STATE, LANES), f32),
            pltpu.VMEM((size, HEAD + share, LANES), bf16),
            pltpu.VMEM((size, HEAD + share, LANES), bf16),
            pltpu.VMEM((size, share, LANES), bf16),
            pltpu.VMEM((size, share, LANES), bf16),
        ]
        + [pltpu.SemaphoreType.DMA((size,))] * 4
        + [pltpu.SemaphoreType.DMA((stages,))] * 2
        + [pltpu.SemaphoreType.DMA((2,))],
        compiler_params=pltpu.CompilerParams(collective_id=0, has_side_effects=True),
        cost_estimate=pl.CostEstimate(
            flops=6 * rows * channels * STATE,
            bytes_accessed=8 * rows * channels,
            transcendentals=rows * channels * STATE,
        ),
        name="first_pass",
    )(rim, mixer_input, step_raw, conv_weight.T, conv_bias[None], rates, bc_rows, rates, key_heads, value_heads)

    entering = entering.reshape(tiles * STATE, LANES)
    mixer_output, pairs = pl.pallas_call(
        second_pass,
        grid=(groups,),
        in_specs=[
            slab,
            slab,
            wide,
            pl.BlockSpec((SUB, LANES), lambda g: (g, 0)),
            rate_spec,
            b_spec,
            c_spec,
            rate_spec,
            pl.BlockSpec(memory_space=pl.ANY),
        ],
        out_specs=[wide, pl.BlockSpec(memory_space=pl.ANY)],
        out_shape=[
            shape((rows, channels), bf16),
            shape((size, rows, 2 * KV_HEADS * HEAD_DIM), bf16),
        ],
        scratch_shapes=[
            pltpu.VMEM((SUB * STATE, LANES), f32),
            pltpu.VMEM((rows * SUB, LANES), f32),
        ]
        + [pltpu.SemaphoreType.DMA((stages,))] * 2
        + [pltpu.SemaphoreType.DMA((1,))],
        compiler_params=pltpu.CompilerParams(collective_id=1, has_side_effects=True),
        cost_estimate=pl.CostEstimate(
            flops=8 * rows * channels * STATE,
            bytes_accessed=12 * rows * channels,
            transcendentals=rows * channels * STATE,
        ),
        name="second_pass",
    )(step, inner, gate_input, skip_gain.reshape(tiles, LANES), rates, bc_rows, bc_rows, entering, some)
    panel = Q_HEADS // KV_HEADS * HEAD_DIM
    keys = rows * size
    pairs = pairs.reshape(keys, 2 * KV_HEADS * HEAD_DIM)
    origin = [int(f"{p:0{stages}b}"[::-1], 2) for p in range(size)]
    key_places = jnp.asarray(
        (np.array(origin)[:, None] * rows + np.arange(rows)).reshape(1, keys), jnp.int32
    )
    attention = pl.pallas_call(
        attend,
        grid=(KV_HEADS,),
        in_specs=[
            pl.BlockSpec(memory_space=pltpu.SMEM),
            pl.BlockSpec((1, keys), lambda g: (0, 0)),
            pl.BlockSpec((rows, panel), lambda g: (0, g)),
            pl.BlockSpec((keys, HEAD_DIM), lambda g: (0, g)),
            pl.BlockSpec((keys, HEAD_DIM), lambda g: (0, KV_HEADS + g)),
        ],
        out_specs=pl.BlockSpec((rows, panel), lambda g: (0, g)),
        out_shape=shape((rows, Q_HEADS * HEAD_DIM), bf16),
        cost_estimate=pl.CostEstimate(
            flops=4 * rows * Q_HEADS * keys * HEAD_DIM,
            bytes_accessed=4 * keys * KV_HEADS * HEAD_DIM,
            transcendentals=rows * Q_HEADS * keys,
        ),
        name="attend",
    )((own * rows).astype(jnp.int32)[None], key_places, query_heads, pairs, pairs)

    return (mixer_output, attention)


def solution(mesh):
    tokens = P(("groups", "ctx"), None)
    in_specs = (tokens,) * 5 + (P(),) * 4 + (tokens,) * 3
    return jax.shard_map(
        per_device, mesh=mesh, in_specs=in_specs, out_specs=(tokens, tokens), check_vma=False
    )
```
